32 devices in a mesh: seq: 8 (over z, y), head: 4 (over x, core).
Axes of the slice: x: 2, y: 2, z: 4, core: 2. Of those that a mesh axis runs over, the one named last changes fastest.
Arguments:
- queries: bfloat16 [8, 1024, 128], P('head', 'seq')
- keys: bfloat16 [8, 1024, 128], P('head', 'seq')
- values: bfloat16 [8, 1024, 128], P('head', 'seq'), may hold values from -6 to 6
- grad_out: bfloat16 [8, 1024, 128], P('head', 'seq'), may hold values from -96 to 96
- rand_ids: int32 [8, 16, 3], P('head', 'seq'), may hold values from 0 to 15, as said below
- global_ids: int32 [2], replicated, may hold values from 0 to 15
Outputs:
- grad_queries: bfloat16 [8, 1024, 128], P('head', 'seq')
- grad_keys: bfloat16 [8, 1024, 128], P('head', 'seq')
- grad_values: bfloat16 [8, 1024, 128], P('head', 'seq')
The draws below stay inside these ranges and needn't reach their ends.
Inputs may be any that keep to these rules, and one draw needn't show every extreme that they name: `rand_ids`: for each head and slot j there is one number M, 0 <= M < 8, such that every query block b names in slot j a block e * 2 + l with e = (b // 2) XOR M and 0 <= l < 2.
All inputs are finite; a program needn't handle non-finite values.
Results may differ from the reference program's by a relative error of at most 0.03.
Values may be sent and summed in bfloat16 or wider, within the bound.
No kernel may reach another device: no remote copies, remote signals or barrier semaphores. Data moves between devices by JAX's collectives and lax.ppermute only.
A program may use at most 64 MiB of HBM per device.

```python
import math
import jax
import jax.numpy as jnp
from jax import lax

HD = 128
BLOCK = 64
GLOBALS = 2
RAND = 3
NB_DEV = 2
HEADS = 8
NBLK = 16
TOKENS = 1024
N_SEQ = 8


def drawn_pair(key):
    shape = (HEADS, TOKENS, HD)
    query_key = jax.random.fold_in(key, 101)
    key_key = jax.random.fold_in(key, 202)
    query_vals = jax.random.normal(query_key, shape, jnp.float32)
    key_vals = jax.random.normal(key_key, shape, jnp.float32)
    return (query_vals, key_vals)


def draw_queries(key, part):
    query_vals, key_vals = drawn_pair(key)
    return query_vals.astype(jnp.bfloat16)


def draw_keys(key, part):
    query_vals, key_vals = drawn_pair(key)
    return key_vals.astype(jnp.bfloat16)


def draw_rand_ids(key, part):
    device_total = NBLK // NB_DEV
    xor_masks = jax.random.randint(jax.random.fold_in(key, 7), (HEADS, RAND), 0, device_total, dtype=jnp.int32)
    xor_masks = xor_masks.at[0, 0].set(device_total - 1)
    local_ids = jax.random.randint(jax.random.fold_in(key, 8), (HEADS, NBLK, RAND), 0, NB_DEV, dtype=jnp.int32)
    local_ids = local_ids.at[0, 0, 0].set(NB_DEV - 1).at[0, NBLK - 1, 0].set(0)
    owner_query = jnp.arange(NBLK, dtype=jnp.int32) // NB_DEV
    target = jnp.bitwise_xor(owner_query[None, :, None], xor_masks[:, None, :])
    return (target * NB_DEV + local_ids).astype(jnp.int32)


def block_levels(key, shape, pieces, least, top_value):
    def one(position, shards_of):
        steps = jax.random.uniform(jax.random.fold_in(jax.random.fold_in(key, 6), position), (shards_of,), jnp.float32, least / len(pieces), top_value / len(pieces))
        return jnp.repeat(jnp.exp(steps), shape[position] // shards_of).reshape((-1,) + (1,) * (len(shape) - position - 1))

    factor_of = one(*pieces[0])
    for cut in pieces[1:]:
        factor_of = factor_of * one(*cut)
    return factor_of


def centred(stream_key, dims, deviation, bound, split=(), kind=jnp.bfloat16):
    level = block_levels(stream_key, dims, split, -0.22, 0.18) if split else 1.0
    drawn = jax.random.normal(stream_key, dims, jnp.float32) * deviation * level
    return jnp.minimum(jnp.maximum(drawn, -bound), bound).astype(kind)


def setup_inputs(seed: int = 0) -> dict:
    streams_of = jax.random.split(jax.random.key(seed), 7)
    return {
        "queries": draw_queries(jax.random.fold_in(streams_of[6], 71), 0),
        "keys": draw_keys(jax.random.fold_in(streams_of[6], 71), 0),
        "values": centred(streams_of[2], (HEADS, TOKENS, HD), 1.0, 6.0, ((0, 4), (1, 8))),
        "grad_out": centred(streams_of[3], (HEADS, TOKENS, HD), 16.0, 96.0, ((0, 4), (1, 8))),
        "rand_ids": draw_rand_ids(jax.random.fold_in(streams_of[6], 71), 0),
        "global_ids": jax.random.randint(streams_of[5], (GLOBALS,), 0, NBLK).astype(jnp.int32),
    }


def one_head(items, global_ids):
    query_rows, key_rows, value_rows, grad_rows, random_ids = items
    slot_total = 3 + GLOBALS + RAND
    fixed_slots = 3 + GLOBALS
    score_scale = 1.0 / math.sqrt(HD)
    query_blocks = query_rows.reshape(NBLK, BLOCK, HD).astype(jnp.float32)
    grad_blocks = grad_rows.reshape(NBLK, BLOCK, HD).astype(jnp.float32)
    key_blocks = key_rows.reshape(NBLK, BLOCK, HD)
    value_blocks = value_rows.reshape(NBLK, BLOCK, HD)
    block_ids = jnp.arange(NBLK, dtype=jnp.int32)
    window_ids = jnp.stack([block_ids - 1, block_ids, block_ids + 1], 1)
    window_valid = (window_ids >= 0) & (window_ids < NBLK)
    window_ids = jnp.clip(window_ids, 0, NBLK - 1).astype(jnp.int32)
    global_cols = jnp.broadcast_to(global_ids[None, :], (NBLK, GLOBALS)).astype(jnp.int32)
    key_index = jnp.concatenate([window_ids, global_cols, random_ids.astype(jnp.int32)], 1)
    valid = jnp.concatenate([window_valid, jnp.ones((NBLK, GLOBALS + RAND), bool)], 1)
    key_list = key_blocks[key_index].reshape(NBLK, slot_total * BLOCK, HD).astype(jnp.float32)
    value_list = value_blocks[key_index].reshape(NBLK, slot_total * BLOCK, HD).astype(jnp.float32)
    mask = jnp.repeat(valid, BLOCK, axis=1)[:, None, :]
    scores = jnp.einsum('nqd,nkd->nqk', query_blocks, key_list) * score_scale
    row_max = lax.optimization_barrier(jnp.max(jnp.where(mask, scores, -1e+30), -1))
    total = lax.optimization_barrier(jnp.sum(jnp.where(mask, jnp.exp(scores - row_max[..., None]), 0.0), -1))
    log_total = row_max + jnp.log(total)
    probs = jnp.where(mask, jnp.exp(scores - log_total[..., None]), 0.0)
    probs_low = probs.astype(jnp.bfloat16).astype(jnp.float32)
    output = jnp.einsum('nqk,nkd->nqd', probs_low, value_list)
    row_dot = lax.optimization_barrier(jnp.sum(grad_blocks * output, -1))
    grad_probs = jnp.einsum('nqd,nkd->nqk', grad_blocks, value_list)
    grad_scores = probs * (grad_probs - row_dot[..., None])
    scores_low = grad_scores.astype(jnp.bfloat16).astype(jnp.float32)
    grad_query = score_scale * jnp.einsum('nqk,nkd->nqd', scores_low, key_list)
    key_terms = score_scale * jnp.einsum('nqk,nqd->nkd', scores_low, query_blocks)
    value_terms = jnp.einsum('nqk,nqd->nkd', probs_low, grad_blocks)
    key_terms = key_terms.reshape(NBLK, slot_total, BLOCK, HD)
    value_terms = value_terms.reshape(NBLK, slot_total, BLOCK, HD)
    grad_key = jnp.zeros((NBLK, BLOCK, HD), jnp.float32).at[key_index[:, :fixed_slots]].add(key_terms[:, :fixed_slots])
    grad_value = jnp.zeros((NBLK, BLOCK, HD), jnp.float32).at[key_index[:, :fixed_slots]].add(value_terms[:, :fixed_slots])
    device_of = (block_ids // NB_DEV).astype(jnp.int32)
    first_blocks = (jnp.arange(N_SEQ, dtype=jnp.int32) * NB_DEV).astype(jnp.int32)
    for slot_index in range(RAND):
        local_of = (random_ids[:, slot_index] % NB_DEV).astype(jnp.int32)
        target = (random_ids[first_blocks, slot_index] // NB_DEV)[:, None] * NB_DEV + jnp.arange(NB_DEV, dtype=jnp.int32)[None, :]
        target = target.reshape(-1).astype(jnp.int32)
        for source, dest_name in ((key_terms, 0), (value_terms, 1)):
            partial_sum = jnp.zeros((N_SEQ, NB_DEV, BLOCK, HD), jnp.float32).at[device_of, local_of].add(source[:, fixed_slots + slot_index])
            rounded = lax.optimization_barrier(partial_sum.astype(jnp.bfloat16)).astype(jnp.float32)
            if dest_name == 0:
                grad_key = grad_key.at[target].add(rounded.reshape(-1, BLOCK, HD))
            else:
                grad_value = grad_value.at[target].add(rounded.reshape(-1, BLOCK, HD))
    return (grad_query.reshape(TOKENS, HD).astype(jnp.bfloat16), grad_key.reshape(TOKENS, HD).astype(jnp.bfloat16), grad_value.reshape(TOKENS, HD).astype(jnp.bfloat16))

def reference(queries, keys, values, grad_out, rand_ids, global_ids):
    grad_queries, grad_keys, grad_values = lax.map(lambda items: one_head(items, global_ids), (queries, keys, values, grad_out, rand_ids))
    return (grad_queries, grad_keys, grad_values)
```

```python
import functools
import math

import jax
import jax.numpy as jnp
from jax import lax
from jax.experimental import pallas as pl
from jax.experimental.pallas import tpu as pltpu
from jax.sharding import PartitionSpec as P

GATHER_BYTES = 8 * 2**20
LOG2E = math.log2(math.e)


def ring_order(count):
    return list(range(0, count, 2)) + list(range(1, count, 2))[::-1]


def dense_kernel(sizes, *refs):
    heads, shards, rows, width, block_rows, slots = sizes
    nk_ref, gcount_ref = refs[0], refs[1]
    a_refs = refs[2 : 2 + shards]
    b_refs = refs[2 + shards : 2 + 2 * shards]
    dq_ref, dk_ref, dv_ref = refs[2 + 2 * shards : 5 + 2 * shards]
    kv, qg, head_buf, ids, bias, s_buf, e_buf, p_buf, sems = refs[5 + 2 * shards :]
    total = shards * rows
    key_blocks = total // block_rows
    own_blocks = rows // block_rows
    scale = 1.0 / math.sqrt(width)
    rate = scale * LOG2E
    copies = []
    for s in range(shards):
        for part in range(2 * heads):
            copies.append(
                pltpu.make_async_copy(
                    a_refs[s].at[pl.ds(part * rows, rows)],
                    kv.at[part, pl.ds(s * rows, rows)],
                    sems.at[0],
                )
            )
            copies.append(
                pltpu.make_async_copy(
                    b_refs[s].at[pl.ds(part * rows, rows)],
                    qg.at[part, pl.ds(s * rows, rows)],
                    sems.at[0],
                )
            )
        copies.append(
            pltpu.make_async_copy(
                a_refs[s].at[pl.ds(2 * heads * rows, head_buf.shape[1])], head_buf.at[s], sems.at[0]
            )
        )
    for c in copies:
        c.start()
    for c in copies:
        c.wait()
    for s in range(shards):
        ids[:, s * rows : (s + 1) * rows] = head_buf[s].astype(jnp.float32)
    nk = nk_ref[...]
    gcount = gcount_ref[...]
    last = heads * slots
    for h in range(heads):
        for s in range(shards):
            lanes = slice(s * rows, (s + 1) * rows)
            nq = ids[last : last + 1, lanes]
            count = gcount + jnp.where(jnp.abs(nk - nq) <= 1.0, 1.0, 0.0)
            for j in range(slots):
                rid = ids[h * slots + j : h * slots + j + 1, lanes]
                count = count + jnp.where(nk == rid, 1.0, 0.0)
            bias[h, :, lanes] = jnp.where(
                count > 0.5, jnp.log(jnp.maximum(count, 1.0)) * (1.0 / scale), -1e30
            )
    dk = [jnp.zeros((rows, width), jnp.float32) for _ in range(heads)]
    dv = [jnp.zeros((rows, width), jnp.float32) for _ in range(heads)]
    pair = 2 * rows
    nt = (((1,), (1,)), ((), ()))
    for pi in range(shards // 2):
        lanes = slice(pi * pair, (pi + 1) * pair)
        for h in range(heads):
            q = qg[h, lanes]
            g = qg[heads + h, lanes]
            s_buf[h, 0] = lax.dot_general(kv[h], q, nt, preferred_element_type=jnp.float32)
            s_buf[h, 1] = lax.dot_general(kv[heads + h], g, nt, preferred_element_type=jnp.float32)
            top = jnp.full((8, pair), -1e30, jnp.float32)
            for kb in range(key_blocks):
                x = s_buf[h, 0, kb * block_rows : (kb + 1) * block_rows] + bias[h, kb : kb + 1, lanes]
                top = jnp.maximum(top, jnp.max(x.reshape(block_rows // 8, 8, pair), axis=0))
            top = jnp.max(top, axis=0, keepdims=True)
            acc_l = jnp.zeros((8, pair), jnp.float32)
            acc_d = jnp.zeros((8, pair), jnp.float32)
            for kb in range(key_blocks):
                rws = slice(kb * block_rows, (kb + 1) * block_rows)
                shift = (bias[h, kb : kb + 1, lanes] - top) * rate
                e = jnp.exp2(s_buf[h, 0, rws] * rate + shift)
                d = e * s_buf[h, 1, rws]
                acc_l = acc_l + jnp.sum(e.reshape(block_rows // 8, 8, pair), axis=0)
                acc_d = acc_d + jnp.sum(d.reshape(block_rows // 8, 8, pair), axis=0)
                if kb < own_blocks:
                    e_buf[h, rws] = e
                elif pi == 0:
                    e_buf[h, rws, 0:rows] = e[:, 0:rows]
            inv = 1.0 / jnp.sum(acc_l, axis=0, keepdims=True)
            dot_row = jnp.sum(acc_d, axis=0, keepdims=True) * inv
            p_own = e_buf[h, 0:rows] * inv
            ds_own = p_own * (s_buf[h, 1, 0:rows] - dot_row)
            dv[h] = dv[h] + jnp.dot(p_own.astype(jnp.bfloat16), g, preferred_element_type=jnp.float32)
            dk[h] = dk[h] + jnp.dot(ds_own.astype(jnp.bfloat16), q, preferred_element_type=jnp.float32)
            if pi == 0:
                for kb in range(key_blocks):
                    rws = slice(kb * block_rows, (kb + 1) * block_rows)
                    ds = e_buf[h, rws, 0:rows] * inv[:, 0:rows]
                    ds = ds * (s_buf[h, 1, rws, 0:rows] - dot_row[:, 0:rows])
                    p_buf[h, rws] = ds.astype(jnp.bfloat16)
                dq = lax.dot_general(
                    p_buf[h], kv[h], (((0,), (0,)), ((), ())), preferred_element_type=jnp.float32
                )
                dq_ref[h] = (dq * scale).astype(dq_ref.dtype)
    for h in range(heads):
        dk_ref[h] = (dk[h] * scale).astype(dk_ref.dtype)
        dv_ref[h] = dv[h].astype(dv_ref.dtype)


def gathered(queries, keys, values, grad_out, rand_ids, global_ids):
    heads, rows, width = queries.shape
    blocks, slots = rand_ids.shape[1:]
    block_rows = rows // blocks
    count = lax.axis_size("seq")
    me = lax.axis_index("seq")
    ring = ring_order(count)
    place = [ring.index(i) for i in range(count)]
    forward = [(ring[i], ring[(i + 1) % count]) for i in range(count)]
    backward = [(b, a) for a, b in forward]
    half = count // 2
    steps = [0]
    for d in range(1, half):
        steps += [-d, d]
    steps.append(half)
    my_place = jnp.asarray(place, jnp.int32)[me]
    owners = jnp.asarray(ring, jnp.int32)[(my_place + jnp.asarray(steps, jnp.int32)) % count]
    nk = (owners[:, None] * blocks + jnp.arange(blocks, dtype=jnp.int32)[None]).reshape(-1, 1)
    gcount = jnp.sum((nk == global_ids[None, :]).astype(jnp.float32), axis=1, keepdims=True)
    nk = jnp.broadcast_to(nk.astype(jnp.float32), (count * blocks, rows))
    gcount = jnp.broadcast_to(gcount, (count * blocks, rows))

    token_ids = jnp.repeat(jnp.moveaxis(rand_ids, 2, 1).reshape(heads * slots, blocks), block_rows, axis=1)
    mine = me * blocks + jnp.arange(rows, dtype=jnp.int32)[None] // block_rows
    head_rows = -(-(heads * slots + 1) // 16) * 16
    header = jnp.concatenate(
        [token_ids, mine, jnp.zeros((head_rows - heads * slots - 1, rows), jnp.int32)]
    ).astype(jnp.bfloat16)
    flat = lambda x: x.reshape(heads * rows, width)
    a = jnp.concatenate([flat(keys), flat(values), header])
    b = jnp.concatenate([flat(queries), flat(grad_out)])
    a_all, b_all = [a], [b]
    af = ab = a
    bf = bb = b
    for _ in range(1, half):
        af, ab = lax.ppermute(af, "seq", forward), lax.ppermute(ab, "seq", backward)
        bf, bb = lax.ppermute(bf, "seq", forward), lax.ppermute(bb, "seq", backward)
        a_all += [af, ab]
        b_all += [bf, bb]
    a_all.append(lax.ppermute(af, "seq", forward))
    b_all.append(lax.ppermute(bb, "seq", backward))

    sizes = (heads, count, rows, width, block_rows, slots)
    total = count * rows
    out = jax.ShapeDtypeStruct(queries.shape, queries.dtype)
    vmem = pl.BlockSpec(memory_space=pltpu.VMEM)
    anyspace = pl.BlockSpec(memory_space=pl.ANY)
    return pl.pallas_call(
        functools.partial(dense_kernel, sizes),
        out_shape=(out, out, out),
        in_specs=[vmem, vmem] + [anyspace] * (2 * count),
        out_specs=(vmem, vmem, vmem),
        scratch_shapes=[
            pltpu.VMEM((2 * heads, total, width), jnp.bfloat16),
            pltpu.VMEM((2 * heads, total, width), jnp.bfloat16),
            pltpu.VMEM((count, head_rows, rows), jnp.bfloat16),
            pltpu.VMEM((head_rows, total), jnp.float32),
            pltpu.VMEM((heads, count * blocks, total), jnp.float32),
            pltpu.VMEM((heads, 2, total, 2 * rows), jnp.float32),
            pltpu.VMEM((heads, total, 2 * rows), jnp.float32),
            pltpu.VMEM((heads, total, rows), jnp.bfloat16),
            pltpu.SemaphoreType.DMA((1,)),
        ],
    )(nk, gcount, *a_all, *b_all)


def with_halo(value, sides, width):
    for axis, dim in sides:
        peers, length = (lax.axis_size(axis), value.shape[dim])
        up = [(i, (i + 1) % peers) for i in range(peers - 1)]
        down = [(j, i) for i, j in up]
        last = lax.slice_in_dim(value, length - width, length, axis=dim)
        initial = lax.slice_in_dim(value, 0, width, axis=dim)
        before = lax.ppermute(last, axis, up)
        after = lax.ppermute(initial, axis, down)
        value = jnp.concatenate([before, value, after], axis=dim)
    return value


def swapped(value, axis, distance):
    mask = 2**distance
    pairs = [(source, source ^ mask) for source in range(lax.axis_size(axis))]
    return lax.ppermute(value, axis, pairs)


def section_list(section_count):
    return list(range(section_count))


def routed(queries, keys, values, grad_out, rand_ids, global_ids):
    head_count, row_count, head_width = queries.shape
    block_count = rand_ids.shape[1]
    slot_count = rand_ids.shape[2]
    block_rows = row_count // block_count
    global_count = global_ids.shape[0]
    slot_total = 3 + global_count + slot_count
    device = lax.axis_index("seq")
    seq_count = lax.axis_size("seq")
    sections = section_list(seq_count.bit_length() - 1)
    score_scale = 1.0 / math.sqrt(head_width)
    key_vals = jnp.stack([keys, values])
    padded = with_halo(key_vals, (("seq", 2),), block_rows)
    padded_blocks = padded.reshape(2, head_count, block_count + 2, block_rows, head_width)
    window = jnp.stack(
        [
            padded_blocks[:, :, 0:block_count],
            padded_blocks[:, :, 1 : block_count + 1],
            padded_blocks[:, :, 2 : block_count + 2],
        ],
        3,
    )
    key_blocks = key_vals.reshape(2, head_count, block_count, block_rows, head_width)
    global_local = global_ids % block_count
    global_owner = global_ids // block_count
    owned = (global_owner == device).astype(jnp.float32)
    picked = jnp.take(key_blocks, global_local, axis=2).astype(jnp.float32)
    global_sum = lax.psum(picked * owned[None, None, :, None, None], "seq")
    global_kv = global_sum.astype(jnp.bfloat16)
    global_keys = jnp.broadcast_to(
        global_kv[:, :, None], (2, head_count, block_count, global_count, block_rows, head_width)
    )
    xor_masks = jnp.bitwise_xor(rand_ids[:, 0, :] // block_count, device)
    pieces = []
    for slot_index in range(slot_count):
        moving = key_vals
        for bit_index in sections:
            arrived = swapped(moving, "seq", bit_index)
            flag_now = jnp.right_shift(xor_masks[:, slot_index], bit_index) & 1 == 1
            moving = jnp.where(flag_now[None, :, None, None], arrived, moving)
        pieces.append(moving)
    routed = jnp.stack(pieces)
    routed_blocks = routed.reshape(slot_count, 2, head_count, block_count, block_rows, head_width)
    random_local = rand_ids % block_count
    local_onehot = (random_local[..., None] == jnp.arange(block_count, dtype=jnp.int32)).astype(
        jnp.bfloat16
    )
    random_keys = jnp.einsum(
        "hqjl,jchlbd->chqjbd", local_onehot, routed_blocks, preferred_element_type=jnp.float32
    ).astype(jnp.bfloat16)
    all_keys = jnp.concatenate([window, global_keys, random_keys], axis=3)
    key_list = all_keys[0].reshape(head_count, block_count, slot_total * block_rows, head_width)
    value_list = all_keys[1].reshape(head_count, block_count, slot_total * block_rows, head_width)
    block_range = jnp.arange(block_count, dtype=jnp.int32)
    left_valid = jnp.logical_not((block_range == 0) & (device == 0))
    right_valid = jnp.logical_not((block_range == block_count - 1) & (device == seq_count - 1))
    valid = jnp.concatenate(
        [
            left_valid[:, None],
            jnp.ones((block_count, 1), bool),
            right_valid[:, None],
            jnp.ones((block_count, global_count + slot_count), bool),
        ],
        1,
    )
    mask = jnp.repeat(valid, block_rows, axis=1)[None, :, None, :]
    query_blocks = queries.reshape(head_count, block_count, block_rows, head_width)
    grad_blocks = grad_out.reshape(head_count, block_count, block_rows, head_width)
    scores = (
        jnp.einsum("hnqd,hnkd->hnqk", query_blocks, key_list, preferred_element_type=jnp.float32)
        * score_scale
    )
    row_max = jnp.max(jnp.where(mask, scores, -1e30), -1)
    total = jnp.sum(jnp.where(mask, jnp.exp(scores - row_max[..., None]), 0.0), -1)
    log_total = row_max + jnp.log(total)
    probs = jnp.where(mask, jnp.exp(scores - log_total[..., None]), 0.0)
    probs_low = probs.astype(jnp.bfloat16)
    output = jnp.einsum(
        "hnqk,hnkd->hnqd", probs_low, value_list, preferred_element_type=jnp.float32
    )
    row_dot = jnp.sum(grad_blocks.astype(jnp.float32) * output, -1)
    grad_probs = jnp.einsum(
        "hnqd,hnkd->hnqk", grad_blocks, value_list, preferred_element_type=jnp.float32
    )
    scores_low = (probs * (grad_probs - row_dot[..., None])).astype(jnp.bfloat16)
    grad_query = score_scale * jnp.einsum(
        "hnqk,hnkd->hnqd", scores_low, key_list, preferred_element_type=jnp.float32
    )
    key_terms = score_scale * jnp.einsum(
        "hnqk,hnqd->hnkd", scores_low, query_blocks, preferred_element_type=jnp.float32
    )
    value_terms = jnp.einsum(
        "hnqk,hnqd->hnkd", probs_low, grad_blocks, preferred_element_type=jnp.float32
    )
    grads = jnp.stack([key_terms, value_terms]).reshape(
        2, head_count, block_count, slot_total, block_rows, head_width
    )
    no_pad = (0, 0)
    frame_sum = jnp.pad(grads[:, :, :, 0], (no_pad, no_pad, (0, 2), no_pad, no_pad))
    frame_sum = frame_sum + jnp.pad(grads[:, :, :, 1], (no_pad, no_pad, (1, 1), no_pad, no_pad))
    frame_sum = frame_sum + jnp.pad(grads[:, :, :, 2], (no_pad, no_pad, (2, 0), no_pad, no_pad))
    own_grads = frame_sum[:, :, 1 : block_count + 1]
    rim_parts = jnp.concatenate([frame_sum[:, :, 0], frame_sum[:, :, block_count + 1]], axis=2)
    rim_back = with_halo(rim_parts.astype(jnp.bfloat16), (("seq", 2),), block_rows).astype(
        rim_parts.dtype
    )
    own_grads = own_grads.at[:, :, 0].add(rim_back[:, :, 0:block_rows])
    own_grads = own_grads.at[:, :, block_count - 1].add(
        rim_back[:, :, 3 * block_rows : 4 * block_rows]
    )
    global_part = jnp.sum(grads[:, :, :, 3 : 3 + global_count], axis=2)
    global_total = lax.psum(global_part, "seq")
    global_onehot = (
        (global_local[:, None] == block_range[None, :]) & (global_owner == device)[:, None]
    ).astype(jnp.float32)
    own_grads = own_grads + jnp.einsum(
        "gn,chgbd->chnbd", global_onehot, global_total, precision=lax.Precision.HIGHEST
    )
    random_part = grads[:, :, :, 3 + global_count :]
    local_float = (random_local[..., None] == block_range).astype(jnp.float32)
    send_back = jnp.einsum(
        "hqjl,chqjbd->jchlbd", local_float, random_part, precision=lax.Precision.HIGHEST
    )
    send_back = send_back.astype(jnp.bfloat16).reshape(
        slot_count, 2, head_count, row_count, head_width
    )
    pieces = []
    for slot_index in range(slot_count):
        moving = send_back[slot_index]
        for bit_index in sections:
            arrived = swapped(moving, "seq", bit_index)
            flag_now = jnp.right_shift(xor_masks[:, slot_index], bit_index) & 1 == 1
            moving = jnp.where(flag_now[None, :, None, None], arrived, moving)
        pieces.append(moving)
    returned = jnp.stack(pieces)
    returned_sum = jnp.sum(returned.astype(jnp.float32), axis=0).reshape(
        2, head_count, block_count, block_rows, head_width
    )
    own_grads = own_grads + returned_sum
    grad_queries = grad_query.reshape(head_count, row_count, head_width).astype(jnp.bfloat16)
    grad_keys = own_grads[0].reshape(head_count, row_count, head_width).astype(jnp.bfloat16)
    grad_values = own_grads[1].reshape(head_count, row_count, head_width).astype(jnp.bfloat16)
    return (grad_queries, grad_keys, grad_values)


def on_device(queries, keys, values, grad_out, rand_ids, global_ids):
    count = lax.axis_size("seq")
    rows, width = queries.shape[1:]
    gathered_bytes = 4 * count * queries.size * queries.dtype.itemsize
    if gathered_bytes <= GATHER_BYTES and count % 2 == 0 and rows == width:
        return gathered(queries, keys, values, grad_out, rand_ids, global_ids)
    return routed(queries, keys, values, grad_out, rand_ids, global_ids)


def solution(mesh):
    in_specs = (
        P("head", "seq", None),
        P("head", "seq", None),
        P("head", "seq", None),
        P("head", "seq", None),
        P("head", "seq", None),
        P(),
    )
    out_specs = (P("head", "seq", None), P("head", "seq", None), P("head", "seq", None))
    return jax.shard_map(
        on_device, mesh=mesh, in_specs=in_specs, out_specs=out_specs, check_vma=False
    )
```

```python
import functools
import math

import jax
import jax.numpy as jnp
from jax import lax
from jax.experimental import pallas as pl
from jax.experimental.pallas import tpu as pltpu
from jax.sharding import PartitionSpec as P

GATHER_BYTES = 8 * 2**20
LOG2E = math.log2(math.e)
NEVER = -1e30
NT = (((1,), (1,)), ((), ()))


def ring_order(count):
    return list(range(0, count, 2)) + list(range(1, count, 2))[::-1]


def pack_kernel(sizes, ids_ref, gids_ref, k_ref, v_ref, q_ref, g_ref, a_ref, b_ref, sems):
    heads, count, rows, width, block_rows, slots, _ = sizes
    blocks = rows // block_rows
    copies = []
    for i, (src, dst, first) in enumerate(
        ((k_ref, a_ref, 0), (v_ref, a_ref, heads), (q_ref, b_ref, 0), (g_ref, b_ref, heads))
    ):
        for h in range(heads):
            copies.append(
                pltpu.make_async_copy(
                    src.at[h], dst.at[pl.ds((first + h) * rows, rows)], sems.at[i * heads + h]
                )
            )
    for c in copies:
        c.start()
    head_rows = a_ref.shape[0] - 2 * heads * rows
    row = lax.broadcasted_iota(jnp.int32, (head_rows, rows), 0)
    lane = lax.broadcasted_iota(jnp.int32, (head_rows, rows), 1)
    me = lax.axis_index("seq")
    block = jnp.zeros_like(lane)
    for n in range(1, blocks):
        block = block + jnp.where(lane >= n * block_rows, 1, 0)
    tile = me * blocks + block
    for h in range(heads):
        for j in range(slots):
            ids = jnp.full_like(lane, ids_ref[h, 0, j])
            for n in range(1, blocks):
                ids = jnp.where(block == n, ids_ref[h, n, j], ids)
            tile = jnp.where(row == h * slots + j, ids, tile)
    for n in range(gids_ref.shape[0]):
        tile = jnp.where(row == heads * slots + 1 + n, gids_ref[n], tile)
    a_ref[2 * heads * rows :] = tile.astype(jnp.float32).astype(jnp.bfloat16)
    for c in copies:
        c.wait()


class Shards:
    def __init__(self, sizes, a_refs, b_refs):
        self.heads, self.count, self.rows, self.width, self.block_rows, self.slots, self.gids = sizes
        self.blocks = self.rows // self.block_rows
        self.a, self.b = a_refs, b_refs
        self.scale = 1.0 / math.sqrt(self.width)
        self.rate = self.scale * LOG2E
        self.heads_of = {s: self.head(s) for s in a_refs}

    def part(self, refs, index, group):
        found = [refs[s][index * self.rows : (index + 1) * self.rows] for s in group]
        return found[0] if len(found) == 1 else jnp.concatenate(found)

    def k(self, h, group):
        return self.part(self.a, h, group)

    def v(self, h, group):
        return self.part(self.a, self.heads + h, group)

    def q(self, h, group):
        return self.part(self.b, h, group)

    def g(self, h, group):
        return self.part(self.b, self.heads + h, group)

    def key_ids(self, group):
        height = len(group) * self.blocks
        row = lax.broadcasted_iota(jnp.int32, (height, self.rows), 0).astype(jnp.float32)
        base = self.heads * self.slots
        nk = jnp.zeros((height, self.rows), jnp.float32)
        for i, s in enumerate(group):
            first = self.heads_of[s][base : base + 1, 0:1] - i * self.blocks
            nk = jnp.where(row >= i * self.blocks, row + first, nk)
        seen = jnp.zeros((height, self.rows), jnp.float32)
        for n in range(self.gids):
            gid = self.heads_of[group[0]][base + 1 + n : base + 2 + n]
            seen = seen + jnp.where(nk == gid, 1.0, 0.0)
        return nk, seen

    def head(self, s):
        return self.a[s][2 * self.heads * self.rows :].astype(jnp.float32)

    def bias(self, keys, group):
        nk, seen = keys
        out = []
        for h in range(self.heads):
            cols = []
            for s in group:
                head = self.heads_of[s]
                nq = head[self.heads * self.slots :][:1]
                count = seen + jnp.where(jnp.abs(nk - nq) <= 1.0, 1.0, 0.0)
                for j in range(self.slots):
                    r = h * self.slots + j
                    count = count + jnp.where(nk == head[r : r + 1], 1.0, 0.0)
                cols.append(jnp.where(count > 0.5, jnp.log2(jnp.maximum(count, 1.0)), NEVER))
            out.append(cols[0] if len(cols) == 1 else jnp.concatenate(cols, axis=1))
        return out

    def scores(self, h, keys, queries):
        return (
            lax.dot_general(self.k(h, keys), self.q(h, queries), NT, preferred_element_type=jnp.float32),
            lax.dot_general(self.v(h, keys), self.g(h, queries), NT, preferred_element_type=jnp.float32),
        )

    def stats(self, scored, bias):
        s, dp = scored
        lanes = s.shape[1]
        steps = self.block_rows // 8
        top = None
        for kb in range(bias.shape[0]):
            x = s[kb * self.block_rows : (kb + 1) * self.block_rows] * self.rate + bias[kb : kb + 1]
            x = jnp.max(x.reshape(steps, 8, lanes), axis=0)
            top = x if top is None else jnp.maximum(top, x)
        top = jnp.maximum(jnp.max(top, axis=0, keepdims=True), 0.5 * NEVER)
        acc_l = acc_d = None
        for kb in range(bias.shape[0]):
            cut = slice(kb * self.block_rows, (kb + 1) * self.block_rows)
            e = jnp.exp2(s[cut] * self.rate + (bias[kb : kb + 1] - top))
            d = jnp.sum((e * dp[cut]).reshape(steps, 8, lanes), axis=0)
            e = jnp.sum(e.reshape(steps, 8, lanes), axis=0)
            acc_l = e if acc_l is None else acc_l + e
            acc_d = d if acc_d is None else acc_d + d
        return top, jnp.sum(acc_l, axis=0, keepdims=True), jnp.sum(acc_d, axis=0, keepdims=True)


def merged(parts):
    if len(parts) == 1:
        return parts[0]
    top = functools.reduce(jnp.maximum, [p[0] for p in parts])
    weights = [jnp.exp2(p[0] - top) for p in parts]
    return top, sum(p[1] * w for p, w in zip(parts, weights)), sum(p[2] * w for p, w in zip(parts, weights))


def rect_stats(sh, keys, queries):
    ids = sh.key_ids(keys)
    found = {}
    pairs = [queries[i : i + 2] for i in range(0, len(queries), 2)]
    for group in pairs:
        bias = sh.bias(ids, group)
        for h in range(sh.heads):
            got = sh.stats(sh.scores(h, keys, group), bias[h])
            for i, s in enumerate(group):
                found[h, s] = tuple(x[:, i * sh.rows : (i + 1) * sh.rows] for x in got)
    return found


def stats_kernel(sizes, slots_in, before, rects, *refs):
    heads = sizes[0]
    n = len(slots_in)
    a_refs = dict(zip(slots_in, refs[:n]))
    b_refs = dict(zip(slots_in, refs[n : 2 * n]))
    rest = refs[2 * n :]
    old = rest[0] if before else None
    out = rest[-1]
    sh = Shards(sizes, a_refs, b_refs)
    parts = {}
    for keys, queries in rects:
        for where, got in rect_stats(sh, keys, queries).items():
            parts.setdefault(where, []).append(got)
    for (h, s), found in parts.items():
        if s in before:
            found.append(tuple(old[s, 3 * h + i : 3 * h + i + 1] for i in range(3)))
        for i, x in enumerate(merged(found)):
            out[s, 3 * h + i : 3 * h + i + 1] = x


def final_kernel(sizes, before, rects, *refs):
    heads, count = sizes[:2]
    a_refs = dict(enumerate(refs[:count]))
    b_refs = dict(enumerate(refs[count : 2 * count]))
    old, dq_ref, dk_ref, dv_ref = refs[2 * count :]
    sh = Shards(sizes, a_refs, b_refs)
    every = list(range(count))
    parts = {}
    for keys, queries in rects:
        for where, got in rect_stats(sh, keys, queries).items():
            parts.setdefault(where, []).append(got)
    shift, dot_row = {}, {}
    for (h, s), found in parts.items():
        if s in before:
            found.append(tuple(old[s, 3 * h + i : 3 * h + i + 1] for i in range(3)))
        top, total, weighted = merged(found)
        shift[h, s] = top + jnp.log2(total)
        dot_row[h, s] = weighted / total
    own_ids, all_ids = sh.key_ids([0]), sh.key_ids(every)
    row_bias = sh.bias(all_ids, [0])
    for h in range(heads):
        dk = dv = None
        for first in range(0, count, 2):
            group = every[first : first + 2]
            bias = sh.bias(own_ids, group)[h]
            s, dp = sh.scores(h, [0], group)
            bias = bias - jnp.concatenate([shift[h, i] for i in group], axis=1)
            dots = jnp.concatenate([dot_row[h, i] for i in group], axis=1)
            p_low, ds_low = weights(sh, s, dp, bias, dots)
            v_term = jnp.dot(p_low, sh.g(h, group), preferred_element_type=jnp.float32)
            k_term = jnp.dot(ds_low, sh.q(h, group), preferred_element_type=jnp.float32)
            dv = v_term if dv is None else dv + v_term
            dk = k_term if dk is None else dk + k_term
        dk_ref[h] = (dk * sh.scale).astype(dk_ref.dtype)
        dv_ref[h] = dv.astype(dv_ref.dtype)
        s, dp = sh.scores(h, every, [0])
        _, ds_low = weights(sh, s, dp, row_bias[h] - shift[h, 0], dot_row[h, 0])
        dq = lax.dot_general(
            ds_low, sh.k(h, every), (((0,), (0,)), ((), ())), preferred_element_type=jnp.float32
        )
        dq_ref[h] = (dq * sh.scale).astype(dq_ref.dtype)


def weights(sh, s, dp, bias, dots):
    p_low, ds_low = [], []
    for kb in range(bias.shape[0]):
        cut = slice(kb * sh.block_rows, (kb + 1) * sh.block_rows)
        p = jnp.exp2(s[cut] * sh.rate + bias[kb : kb + 1])
        p_low.append(p.astype(jnp.bfloat16))
        ds_low.append((p * (dp[cut] - dots)).astype(jnp.bfloat16))
    return jnp.concatenate(p_low), jnp.concatenate(ds_low)


def near(arrays):
    return [pltpu.with_memory_space_constraint(x, pltpu.VMEM) for x in arrays]


def gathered(queries, keys, values, grad_out, rand_ids, global_ids):
    heads, rows, width = queries.shape
    blocks, slots = rand_ids.shape[1:]
    count = lax.axis_size("seq")
    ring = ring_order(count)
    forward = [(ring[i], ring[(i + 1) % count]) for i in range(count)]
    backward = [(b, a) for a, b in forward]
    half = count // 2
    sizes = (heads, count, rows, width, rows // blocks, slots, global_ids.shape[0])
    head_rows = -(-(heads * slots + 1 + global_ids.shape[0]) // 16) * 16
    vmem = pl.BlockSpec(memory_space=pltpu.VMEM)
    smem = pl.BlockSpec(memory_space=pltpu.SMEM)
    anyspace = pl.BlockSpec(memory_space=pl.ANY)
    a, b = pl.pallas_call(
        functools.partial(pack_kernel, sizes),
        out_shape=(
            pltpu.VMEM((2 * heads * rows + head_rows, width), queries.dtype),
            pltpu.VMEM((2 * heads * rows, width), queries.dtype),
        ),
        in_specs=[smem, smem] + [anyspace] * 4,
        out_specs=(vmem, vmem),
        scratch_shapes=[pltpu.SemaphoreType.DMA((4 * heads,))],
    )(rand_ids, global_ids, keys, values, queries, grad_out)

    a_all, b_all = [a], [b]
    af = ab = a
    bf = bb = b
    stat = None
    stat_shape = pltpu.VMEM((count, 8, rows), jnp.float32)
    for d in range(1, half):
        af, ab = lax.ppermute(af, "seq", forward), lax.ppermute(ab, "seq", backward)
        bf, bb = lax.ppermute(bf, "seq", forward), lax.ppermute(bb, "seq", backward)
        a_all += [af, ab]
        b_all += [bf, bb]
        if d < half - 2:
            continue
        now = list(range(2 * d + 1))
        if stat is None:
            before, rects = [], [(now, now)]
        else:
            before, new = now[:-2], now[-2:]
            rects = [(new, before), (now, new)]
        stat = pl.pallas_call(
            functools.partial(stats_kernel, sizes, now, before, rects),
            out_shape=stat_shape,
            in_specs=[vmem] * (2 * len(now) + bool(before)),
            out_specs=vmem,
            cost_estimate=pl.CostEstimate(flops=10**9, bytes_accessed=10**6, transcendentals=10**6),
        )(*near(a_all), *near(b_all), *near([stat] if before else []))
    a_all.append(lax.ppermute(af, "seq", forward))
    b_all.append(lax.ppermute(bb, "seq", backward))
    every = list(range(count))
    before = every[:-1]
    rects = [(every[-1:], before), (every, every[-1:])]
    out = jax.ShapeDtypeStruct(queries.shape, queries.dtype)
    return pl.pallas_call(
        functools.partial(final_kernel, sizes, before, rects),
        out_shape=(out, out, out),
        in_specs=[vmem] * (2 * count + 1),
        out_specs=(vmem, vmem, vmem),
    )(*near(a_all), *near(b_all), *near([stat]))


def with_halo(value, sides, width):
    for axis, dim in sides:
        peers, length = (lax.axis_size(axis), value.shape[dim])
        up = [(i, (i + 1) % peers) for i in range(peers - 1)]
        down = [(j, i) for i, j in up]
        last = lax.slice_in_dim(value, length - width, length, axis=dim)
        initial = lax.slice_in_dim(value, 0, width, axis=dim)
        before = lax.ppermute(last, axis, up)
        after = lax.ppermute(initial, axis, down)
        value = jnp.concatenate([before, value, after], axis=dim)
    return value


def swapped(value, axis, distance):
    mask = 2**distance
    pairs = [(source, source ^ mask) for source in range(lax.axis_size(axis))]
    return lax.ppermute(value, axis, pairs)


def section_list(section_count):
    return list(range(section_count))


def routed(queries, keys, values, grad_out, rand_ids, global_ids):
    head_count, row_count, head_width = queries.shape
    block_count = rand_ids.shape[1]
    slot_count = rand_ids.shape[2]
    block_rows = row_count // block_count
    global_count = global_ids.shape[0]
    slot_total = 3 + global_count + slot_count
    device = lax.axis_index("seq")
    seq_count = lax.axis_size("seq")
    sections = section_list(seq_count.bit_length() - 1)
    score_scale = 1.0 / math.sqrt(head_width)
    key_vals = jnp.stack([keys, values])
    padded = with_halo(key_vals, (("seq", 2),), block_rows)
    padded_blocks = padded.reshape(2, head_count, block_count + 2, block_rows, head_width)
    window = jnp.stack(
        [
            padded_blocks[:, :, 0:block_count],
            padded_blocks[:, :, 1 : block_count + 1],
            padded_blocks[:, :, 2 : block_count + 2],
        ],
        3,
    )
    key_blocks = key_vals.reshape(2, head_count, block_count, block_rows, head_width)
    global_local = global_ids % block_count
    global_owner = global_ids // block_count
    owned = (global_owner == device).astype(jnp.float32)
    picked = jnp.take(key_blocks, global_local, axis=2).astype(jnp.float32)
    global_sum = lax.psum(picked * owned[None, None, :, None, None], "seq")
    global_kv = global_sum.astype(jnp.bfloat16)
    global_keys = jnp.broadcast_to(
        global_kv[:, :, None], (2, head_count, block_count, global_count, block_rows, head_width)
    )
    xor_masks = jnp.bitwise_xor(rand_ids[:, 0, :] // block_count, device)
    pieces = []
    for slot_index in range(slot_count):
        moving = key_vals
        for bit_index in sections:
            arrived = swapped(moving, "seq", bit_index)
            flag_now = jnp.right_shift(xor_masks[:, slot_index], bit_index) & 1 == 1
            moving = jnp.where(flag_now[None, :, None, None], arrived, moving)
        pieces.append(moving)
    routed = jnp.stack(pieces)
    routed_blocks = routed.reshape(slot_count, 2, head_count, block_count, block_rows, head_width)
    random_local = rand_ids % block_count
    local_onehot = (random_local[..., None] == jnp.arange(block_count, dtype=jnp.int32)).astype(
        jnp.bfloat16
    )
    random_keys = jnp.einsum(
        "hqjl,jchlbd->chqjbd", local_onehot, routed_blocks, preferred_element_type=jnp.float32
    ).astype(jnp.bfloat16)
    all_keys = jnp.concatenate([window, global_keys, random_keys], axis=3)
    key_list = all_keys[0].reshape(head_count, block_count, slot_total * block_rows, head_width)
    value_list = all_keys[1].reshape(head_count, block_count, slot_total * block_rows, head_width)
    block_range = jnp.arange(block_count, dtype=jnp.int32)
    left_valid = jnp.logical_not((block_range == 0) & (device == 0))
    right_valid = jnp.logical_not((block_range == block_count - 1) & (device == seq_count - 1))
    valid = jnp.concatenate(
        [
            left_valid[:, None],
            jnp.ones((block_count, 1), bool),
            right_valid[:, None],
            jnp.ones((block_count, global_count + slot_count), bool),
        ],
        1,
    )
    mask = jnp.repeat(valid, block_rows, axis=1)[None, :, None, :]
    query_blocks = queries.reshape(head_count, block_count, block_rows, head_width)
    grad_blocks = grad_out.reshape(head_count, block_count, block_rows, head_width)
    scores = (
        jnp.einsum("hnqd,hnkd->hnqk", query_blocks, key_list, preferred_element_type=jnp.float32)
        * score_scale
    )
    row_max = jnp.max(jnp.where(mask, scores, -1e30), -1)
    total = jnp.sum(jnp.where(mask, jnp.exp(scores - row_max[..., None]), 0.0), -1)
    log_total = row_max + jnp.log(total)
    probs = jnp.where(mask, jnp.exp(scores - log_total[..., None]), 0.0)
    probs_low = probs.astype(jnp.bfloat16)
    output = jnp.einsum(
        "hnqk,hnkd->hnqd", probs_low, value_list, preferred_element_type=jnp.float32
    )
    row_dot = jnp.sum(grad_blocks.astype(jnp.float32) * output, -1)
    grad_probs = jnp.einsum(
        "hnqd,hnkd->hnqk", grad_blocks, value_list, preferred_element_type=jnp.float32
    )
    scores_low = (probs * (grad_probs - row_dot[..., None])).astype(jnp.bfloat16)
    grad_query = score_scale * jnp.einsum(
        "hnqk,hnkd->hnqd", scores_low, key_list, preferred_element_type=jnp.float32
    )
    key_terms = score_scale * jnp.einsum(
        "hnqk,hnqd->hnkd", scores_low, query_blocks, preferred_element_type=jnp.float32
    )
    value_terms = jnp.einsum(
        "hnqk,hnqd->hnkd", probs_low, grad_blocks, preferred_element_type=jnp.float32
    )
    grads = jnp.stack([key_terms, value_terms]).reshape(
        2, head_count, block_count, slot_total, block_rows, head_width
    )
    no_pad = (0, 0)
    frame_sum = jnp.pad(grads[:, :, :, 0], (no_pad, no_pad, (0, 2), no_pad, no_pad))
    frame_sum = frame_sum + jnp.pad(grads[:, :, :, 1], (no_pad, no_pad, (1, 1), no_pad, no_pad))
    frame_sum = frame_sum + jnp.pad(grads[:, :, :, 2], (no_pad, no_pad, (2, 0), no_pad, no_pad))
    own_grads = frame_sum[:, :, 1 : block_count + 1]
    rim_parts = jnp.concatenate([frame_sum[:, :, 0], frame_sum[:, :, block_count + 1]], axis=2)
    rim_back = with_halo(rim_parts.astype(jnp.bfloat16), (("seq", 2),), block_rows).astype(
        rim_parts.dtype
    )
    own_grads = own_grads.at[:, :, 0].add(rim_back[:, :, 0:block_rows])
    own_grads = own_grads.at[:, :, block_count - 1].add(
        rim_back[:, :, 3 * block_rows : 4 * block_rows]
    )
    global_part = jnp.sum(grads[:, :, :, 3 : 3 + global_count], axis=2)
    global_total = lax.psum(global_part, "seq")
    global_onehot = (
        (global_local[:, None] == block_range[None, :]) & (global_owner == device)[:, None]
    ).astype(jnp.float32)
    own_grads = own_grads + jnp.einsum(
        "gn,chgbd->chnbd", global_onehot, global_total, precision=lax.Precision.HIGHEST
    )
    random_part = grads[:, :, :, 3 + global_count :]
    local_float = (random_local[..., None] == block_range).astype(jnp.float32)
    send_back = jnp.einsum(
        "hqjl,chqjbd->jchlbd", local_float, random_part, precision=lax.Precision.HIGHEST
    )
    send_back = send_back.astype(jnp.bfloat16).reshape(
        slot_count, 2, head_count, row_count, head_width
    )
    pieces = []
    for slot_index in range(slot_count):
        moving = send_back[slot_index]
        for bit_index in sections:
            arrived = swapped(moving, "seq", bit_index)
            flag_now = jnp.right_shift(xor_masks[:, slot_index], bit_index) & 1 == 1
            moving = jnp.where(flag_now[None, :, None, None], arrived, moving)
        pieces.append(moving)
    returned = jnp.stack(pieces)
    returned_sum = jnp.sum(returned.astype(jnp.float32), axis=0).reshape(
        2, head_count, block_count, block_rows, head_width
    )
    own_grads = own_grads + returned_sum
    grad_queries = grad_query.reshape(head_count, row_count, head_width).astype(jnp.bfloat16)
    grad_keys = own_grads[0].reshape(head_count, row_count, head_width).astype(jnp.bfloat16)
    grad_values = own_grads[1].reshape(head_count, row_count, head_width).astype(jnp.bfloat16)
    return (grad_queries, grad_keys, grad_values)


def on_device(queries, keys, values, grad_out, rand_ids, global_ids):
    count = lax.axis_size("seq")
    rows, width = queries.shape[1:]
    gathered_bytes = 4 * count * queries.size * queries.dtype.itemsize
    if gathered_bytes <= GATHER_BYTES and count % 2 == 0 and rows == width:
        return gathered(queries, keys, values, grad_out, rand_ids, global_ids)
    return routed(queries, keys, values, grad_out, rand_ids, global_ids)


def solution(mesh):
    in_specs = (
        P("head", "seq", None),
        P("head", "seq", None),
        P("head", "seq", None),
        P("head", "seq", None),
        P("head", "seq", None),
        P(),
    )
    out_specs = (P("head", "seq", None), P("head", "seq", None), P("head", "seq", None))
    return jax.shard_map(
        on_device, mesh=mesh, in_specs=in_specs, out_specs=out_specs, check_vma=False
    )
```

```python
import functools
import math

import jax
import jax.numpy as jnp
from jax import lax
from jax.experimental import pallas as pl
from jax.experimental.pallas import tpu as pltpu
from jax.sharding import PartitionSpec as P

GATHER_BYTES = 8 * 2**20
KERNEL_VMEM = 16 * 2**20
LOG2E = math.log2(math.e)
NEVER = -1e30
NT = (((1,), (1,)), ((), ()))


def ring_order(count):
    return list(range(0, count, 2)) + list(range(1, count, 2))[::-1]


def pack_kernel(sizes, ids_hbm, gids_hbm, k_ref, v_ref, q_ref, g_ref, a_ref, b_ref, ids_ref, gids_ref, sems):
    heads, count, rows, width, block_rows, slots, _ = sizes
    blocks = rows // block_rows
    small = [
        pltpu.make_async_copy(ids_hbm, ids_ref, sems.at[0]),
        pltpu.make_async_copy(gids_hbm, gids_ref, sems.at[1]),
    ]
    copies = []
    for i, (src, dst, first) in enumerate(
        ((k_ref, a_ref, 0), (v_ref, a_ref, heads), (q_ref, b_ref, 0), (g_ref, b_ref, heads))
    ):
        for h in range(heads):
            copies.append(
                pltpu.make_async_copy(
                    src.at[h], dst.at[pl.ds((first + h) * rows, rows)], sems.at[2 + i * heads + h]
                )
            )
    for c in small + copies:
        c.start()
    head_rows = a_ref.shape[0] - 2 * heads * rows
    row = lax.broadcasted_iota(jnp.int32, (head_rows, rows), 0)
    lane = lax.broadcasted_iota(jnp.int32, (head_rows, rows), 1)
    me = lax.axis_index("seq")
    block = jnp.zeros_like(lane)
    for n in range(1, blocks):
        block = block + jnp.where(lane >= n * block_rows, 1, 0)
    tile = me * blocks + block
    for c in small:
        c.wait()
    for h in range(heads):
        for j in range(slots):
            ids = jnp.full_like(lane, ids_ref[h, 0, j])
            for n in range(1, blocks):
                ids = jnp.where(block == n, ids_ref[h, n, j], ids)
            tile = jnp.where(row == h * slots + j, ids, tile)
    for n in range(gids_ref.shape[0]):
        tile = jnp.where(row == heads * slots + 1 + n, gids_ref[n], tile)
    a_ref[2 * heads * rows :] = tile.astype(jnp.float32).astype(jnp.bfloat16)
    for c in copies:
        c.wait()


class Shards:
    def __init__(self, sizes, a_refs, b_refs):
        self.heads, self.count, self.rows, self.width, self.block_rows, self.slots, self.gids = sizes
        self.blocks = self.rows // self.block_rows
        self.a, self.b = a_refs, b_refs
        self.scale = 1.0 / math.sqrt(self.width)
        self.rate = self.scale * LOG2E
        self.heads_of = {s: self.head(s) for s in a_refs}

    def part(self, refs, index, group):
        found = [refs[s][index * self.rows : (index + 1) * self.rows] for s in group]
        return found[0] if len(found) == 1 else jnp.concatenate(found)

    def k(self, h, group):
        return self.part(self.a, h, group)

    def v(self, h, group):
        return self.part(self.a, self.heads + h, group)

    def q(self, h, group):
        return self.part(self.b, h, group)

    def g(self, h, group):
        return self.part(self.b, self.heads + h, group)

    def key_ids(self, group):
        height = len(group) * self.blocks
        row = lax.broadcasted_iota(jnp.int32, (height, self.rows), 0).astype(jnp.float32)
        base = self.heads * self.slots
        nk = jnp.zeros((height, self.rows), jnp.float32)
        for i, s in enumerate(group):
            first = self.heads_of[s][base : base + 1, 0:1] - i * self.blocks
            nk = jnp.where(row >= i * self.blocks, row + first, nk)
        seen = jnp.zeros((height, self.rows), jnp.float32)
        for n in range(self.gids):
            gid = self.heads_of[group[0]][base + 1 + n : base + 2 + n]
            seen = seen + jnp.where(nk == gid, 1.0, 0.0)
        return nk, seen

    def head(self, s):
        return self.a[s][2 * self.heads * self.rows :].astype(jnp.float32)

    def bias(self, keys, group):
        nk, seen = keys
        out = []
        for h in range(self.heads):
            cols = []
            for s in group:
                head = self.heads_of[s]
                nq = head[self.heads * self.slots :][:1]
                count = seen + jnp.where(jnp.abs(nk - nq) <= 1.0, 1.0, 0.0)
                for j in range(self.slots):
                    r = h * self.slots + j
                    count = count + jnp.where(nk == head[r : r + 1], 1.0, 0.0)
                cols.append(jnp.where(count > 0.5, jnp.log2(jnp.maximum(count, 1.0)), NEVER))
            out.append(cols[0] if len(cols) == 1 else jnp.concatenate(cols, axis=1))
        return out

    def scores(self, h, keys, queries):
        return (
            lax.dot_general(self.k(h, keys), self.q(h, queries), NT, preferred_element_type=jnp.float32),
            lax.dot_general(self.v(h, keys), self.g(h, queries), NT, preferred_element_type=jnp.float32),
        )

    def stats(self, scored, bias, keep):
        s, dp = scored
        lanes = s.shape[1]
        steps = self.block_rows // 8
        top = None
        for kb in range(bias.shape[0]):
            x = s[kb * self.block_rows : (kb + 1) * self.block_rows] * self.rate + bias[kb : kb + 1]
            x = jnp.max(x.reshape(steps, 8, lanes), axis=0)
            top = x if top is None else jnp.maximum(top, x)
        top = jnp.maximum(jnp.max(top, axis=0, keepdims=True), 0.5 * NEVER)
        acc_l = acc_d = None
        for kb in range(bias.shape[0]):
            cut = slice(kb * self.block_rows, (kb + 1) * self.block_rows)
            e = jnp.exp2(s[cut] * self.rate + (bias[kb : kb + 1] - top))
            keep(kb, cut, e, dp[cut])
            d = jnp.sum((e * dp[cut]).reshape(steps, 8, lanes), axis=0)
            e = jnp.sum(e.reshape(steps, 8, lanes), axis=0)
            acc_l = e if acc_l is None else acc_l + e
            acc_d = d if acc_d is None else acc_d + d
        return top, jnp.sum(acc_l, axis=0, keepdims=True), jnp.sum(acc_d, axis=0, keepdims=True)


def rect_shapes(sizes, keys, queries, wrap):
    heads, rows = sizes[0], sizes[2]
    shapes = [wrap((heads * 8, len(queries) * rows), jnp.float32)]
    if 0 in keys:
        shapes += [wrap((heads, rows, len(queries) * rows), jnp.float32)] * 2
    if 0 in queries:
        shapes += [wrap((heads, len(keys) * rows, rows), jnp.float32)] * 2
    return shapes


def rect_refs(refs, keys, queries):
    refs = list(refs)
    stat = refs.pop(0)
    cols = (refs.pop(0), refs.pop(0)) if 0 in keys else None
    rest = (refs.pop(0), refs.pop(0)) if 0 in queries else None
    return stat, cols, rest


def run_rect(sh, keys, queries, refs):
    stat, cols, mine = rect_refs(refs, keys, queries)
    ids = sh.key_ids(keys)
    own = keys.index(0) * sh.blocks if 0 in keys else None
    for first in range(0, len(queries), 2):
        group = queries[first : first + 2]
        lanes = slice(first * sh.rows, (first + len(group)) * sh.rows)
        bias = sh.bias(ids, group)
        scored = [sh.scores(h, keys, group) for h in range(sh.heads)]
        for h in range(sh.heads):

            def keep(kb, cut, e, dp):
                if own is not None and own <= kb < own + sh.blocks:
                    part = slice((kb - own) * sh.block_rows, (kb - own + 1) * sh.block_rows)
                    cols[0][h, part, lanes] = e
                    cols[1][h, part, lanes] = dp
                if 0 in group:
                    place = slice(group.index(0) * sh.rows, (group.index(0) + 1) * sh.rows)
                    mine[0][h, cut] = e[:, place]
                    mine[1][h, cut] = dp[:, place]

            for i, x in enumerate(sh.stats(scored[h], bias[h], keep)):
                stat[8 * h + i : 8 * h + i + 1, lanes] = x


def stats_kernel(sizes, slots_in, rects, *refs):
    n = len(slots_in)
    sh = Shards(sizes, dict(zip(slots_in, refs[:n])), dict(zip(slots_in, refs[n : 2 * n])))
    rest = refs[2 * n :]
    for keys, queries in rects:
        size = len(rect_shapes(sizes, keys, queries, lambda *x: None))
        run_rect(sh, keys, queries, rest[:size])
        rest = rest[size:]


def final_kernel(sizes, done, rects, *refs):
    heads, count, rows = sizes[:3]
    blocks = rows // sizes[4]
    sh = Shards(sizes, dict(enumerate(refs[:count])), dict(enumerate(refs[count : 2 * count])))
    rest = refs[2 * count :]
    known = []
    outputs = []
    for group in (done, rects):
        for keys, queries in group:
            size = len(rect_shapes(sizes, keys, queries, lambda *x: None))
            known.append((keys, queries, rect_refs(rest[:size], keys, queries)))
            if group is rects:
                run_rect(sh, keys, queries, rest[:size])
            rest = rest[size:]
        if group is done:
            outputs, rest = rest[:3], rest[3:]
    dq_ref, dk_ref, dv_ref = outputs
    dq_buf, dk_buf, dv_buf, sems = rest

    def part(found, h, i, s):
        keys, queries, (stat, _, _) = found
        lanes = slice(queries.index(s) * rows, (queries.index(s) + 1) * rows)
        return stat[8 * h + i : 8 * h + i + 1, lanes]

    shift, dot_row = {}, {}
    for h in range(heads):
        for s in range(count):
            holds = [k for k in known if s in k[1]]
            top = functools.reduce(jnp.maximum, [part(k, h, 0, s) for k in holds])
            scales = [jnp.exp2(part(k, h, 0, s) - top) for k in holds]
            total = sum(part(k, h, 1, s) * w for k, w in zip(holds, scales))
            shift[h, s] = top + jnp.log2(total)
            dot_row[h, s] = sum(part(k, h, 2, s) * w for k, w in zip(holds, scales)) / total

    def weight(found, h, s):
        return jnp.exp2(part(found, h, 0, s) - shift[h, s])

    copies = []

    def send(h, i, src, dst):
        copies.append(pltpu.make_async_copy(src.at[h], dst.at[h], sems.at[3 * h + i]))
        copies[-1].start()

    steps = range(0, rows, sizes[4])
    for h in range(heads):
        order, low = [], []
        for k in known:
            keys, queries, (_, _, mine) = k
            if 0 not in queries:
                continue
            order += keys
            w = weight(k, h, 0)
            for r in range(0, len(keys) * rows, sizes[4]):
                cut = slice(r, r + sizes[4])
                low.append(((mine[0][h, cut] * w) * (mine[1][h, cut] - dot_row[h, 0])).astype(jnp.bfloat16))
        dq = lax.dot_general(
            jnp.concatenate(low), sh.k(h, order), (((0,), (0,)), ((), ())),
            preferred_element_type=jnp.float32,
        )
        dq_buf[h] = (dq * sh.scale).astype(dq_buf.dtype)
        send(h, 0, dq_buf, dq_ref)
    for h in range(heads):
        order, p_low, ds_low = [], [], []
        for k in known:
            keys, queries, (_, cols, _) = k
            if 0 not in keys:
                continue
            for s in queries:
                order.append(s)
                lanes = slice(queries.index(s) * rows, (queries.index(s) + 1) * rows)
                w, dots = weight(k, h, s), dot_row[h, s]
                p_col, ds_col = [], []
                for r in steps:
                    p = cols[0][h, r : r + sizes[4], lanes] * w
                    p_col.append(p.astype(jnp.bfloat16))
                    ds_col.append((p * (cols[1][h, r : r + sizes[4], lanes] - dots)).astype(jnp.bfloat16))
                p_low.append(jnp.concatenate(p_col))
                ds_low.append(jnp.concatenate(ds_col))
        dv = jnp.dot(jnp.concatenate(p_low, axis=1), sh.g(h, order), preferred_element_type=jnp.float32)
        dv_buf[h] = dv.astype(dv_buf.dtype)
        send(h, 2, dv_buf, dv_ref)
        dk = jnp.dot(jnp.concatenate(ds_low, axis=1), sh.q(h, order), preferred_element_type=jnp.float32)
        dk_buf[h] = (dk * sh.scale).astype(dk_buf.dtype)
        send(h, 1, dk_buf, dk_ref)
    for c in copies:
        c.wait()


def near(arrays):
    return [pltpu.with_memory_space_constraint(x, pltpu.VMEM) for x in arrays]


def gathered(queries, keys, values, grad_out, rand_ids, global_ids):
    heads, rows, width = queries.shape
    blocks, slots = rand_ids.shape[1:]
    count = lax.axis_size("seq")
    ring = ring_order(count)
    forward = [(ring[i], ring[(i + 1) % count]) for i in range(count)]
    backward = [(b, a) for a, b in forward]
    half = count // 2
    sizes = (heads, count, rows, width, rows // blocks, slots, global_ids.shape[0])
    head_rows = -(-(heads * slots + 1 + global_ids.shape[0]) // 16) * 16
    vmem = pl.BlockSpec(memory_space=pltpu.VMEM)
    anyspace = pl.BlockSpec(memory_space=pl.ANY)
    a, b = pl.pallas_call(
        functools.partial(pack_kernel, sizes),
        out_shape=(
            pltpu.VMEM((2 * heads * rows + head_rows, width), queries.dtype),
            pltpu.VMEM((2 * heads * rows, width), queries.dtype),
        ),
        in_specs=[anyspace] * 6,
        out_specs=(vmem, vmem),
        scratch_shapes=[
            pltpu.SMEM(rand_ids.shape, jnp.int32),
            pltpu.SMEM(global_ids.shape, jnp.int32),
            pltpu.SemaphoreType.DMA((2 + 4 * heads,)),
        ],
    )(rand_ids, global_ids, keys, values, queries, grad_out)

    a_all, b_all = [a], [b]
    af = ab = a
    bf = bb = b
    done, left = [], []
    for d in range(1, half):
        af, ab = lax.ppermute(af, "seq", forward), lax.ppermute(ab, "seq", backward)
        bf, bb = lax.ppermute(bf, "seq", forward), lax.ppermute(bb, "seq", backward)
        a_all += [af, ab]
        b_all += [bf, bb]
        if d < half - 2:
            continue
        now = list(range(2 * d + 1))
        rects = [(now[-2:], now[:-2]), (now, now[-2:])] if done else [(now, now)]
        shapes = [x for r in rects for x in rect_shapes(sizes, *r, pltpu.VMEM)]
        got = pl.pallas_call(
            functools.partial(stats_kernel, sizes, now, rects),
            out_shape=tuple(shapes),
            compiler_params=pltpu.CompilerParams(vmem_limit_bytes=KERNEL_VMEM),
            in_specs=[vmem] * (2 * len(now)),
            out_specs=(vmem,) * len(shapes),
            cost_estimate=pl.CostEstimate(flops=10**9, bytes_accessed=10**6, transcendentals=10**6),
        )(*near(a_all), *near(b_all))
        done += rects
        left += got
    a_all.append(lax.ppermute(af, "seq", forward))
    b_all.append(lax.ppermute(bb, "seq", backward))
    every = list(range(count))
    rects = [(every[-1:], every[:-1]), (every, every[-1:])]
    out = jax.ShapeDtypeStruct(queries.shape, queries.dtype)
    buf = pltpu.VMEM(queries.shape, queries.dtype)
    return pl.pallas_call(
        functools.partial(final_kernel, sizes, done, rects),
        out_shape=(out, out, out),
        compiler_params=pltpu.CompilerParams(vmem_limit_bytes=KERNEL_VMEM),
        in_specs=[vmem] * (2 * count + len(left)),
        out_specs=(anyspace,) * 3,
        scratch_shapes=[x for r in rects for x in rect_shapes(sizes, *r, pltpu.VMEM)]
        + [buf, buf, buf, pltpu.SemaphoreType.DMA((3 * heads,))],
    )(*near(a_all), *near(b_all), *near(left))


def with_halo(value, sides, width):
    for axis, dim in sides:
        peers, length = (lax.axis_size(axis), value.shape[dim])
        up = [(i, (i + 1) % peers) for i in range(peers - 1)]
        down = [(j, i) for i, j in up]
        last = lax.slice_in_dim(value, length - width, length, axis=dim)
        initial = lax.slice_in_dim(value, 0, width, axis=dim)
        before = lax.ppermute(last, axis, up)
        after = lax.ppermute(initial, axis, down)
        value = jnp.concatenate([before, value, after], axis=dim)
    return value


def swapped(value, axis, distance):
    mask = 2**distance
    pairs = [(source, source ^ mask) for source in range(lax.axis_size(axis))]
    return lax.ppermute(value, axis, pairs)


def section_list(section_count):
    return list(range(section_count))


def routed(queries, keys, values, grad_out, rand_ids, global_ids):
    head_count, row_count, head_width = queries.shape
    block_count = rand_ids.shape[1]
    slot_count = rand_ids.shape[2]
    block_rows = row_count // block_count
    global_count = global_ids.shape[0]
    slot_total = 3 + global_count + slot_count
    device = lax.axis_index("seq")
    seq_count = lax.axis_size("seq")
    sections = section_list(seq_count.bit_length() - 1)
    score_scale = 1.0 / math.sqrt(head_width)
    key_vals = jnp.stack([keys, values])
    padded = with_halo(key_vals, (("seq", 2),), block_rows)
    padded_blocks = padded.reshape(2, head_count, block_count + 2, block_rows, head_width)
    window = jnp.stack(
        [
            padded_blocks[:, :, 0:block_count],
            padded_blocks[:, :, 1 : block_count + 1],
            padded_blocks[:, :, 2 : block_count + 2],
        ],
        3,
    )
    key_blocks = key_vals.reshape(2, head_count, block_count, block_rows, head_width)
    global_local = global_ids % block_count
    global_owner = global_ids // block_count
    owned = (global_owner == device).astype(jnp.float32)
    picked = jnp.take(key_blocks, global_local, axis=2).astype(jnp.float32)
    global_sum = lax.psum(picked * owned[None, None, :, None, None], "seq")
    global_kv = global_sum.astype(jnp.bfloat16)
    global_keys = jnp.broadcast_to(
        global_kv[:, :, None], (2, head_count, block_count, global_count, block_rows, head_width)
    )
    xor_masks = jnp.bitwise_xor(rand_ids[:, 0, :] // block_count, device)
    pieces = []
    for slot_index in range(slot_count):
        moving = key_vals
        for bit_index in sections:
            arrived = swapped(moving, "seq", bit_index)
            flag_now = jnp.right_shift(xor_masks[:, slot_index], bit_index) & 1 == 1
            moving = jnp.where(flag_now[None, :, None, None], arrived, moving)
        pieces.append(moving)
    routed = jnp.stack(pieces)
    routed_blocks = routed.reshape(slot_count, 2, head_count, block_count, block_rows, head_width)
    random_local = rand_ids % block_count
    local_onehot = (random_local[..., None] == jnp.arange(block_count, dtype=jnp.int32)).astype(
        jnp.bfloat16
    )
    random_keys = jnp.einsum(
        "hqjl,jchlbd->chqjbd", local_onehot, routed_blocks, preferred_element_type=jnp.float32
    ).astype(jnp.bfloat16)
    all_keys = jnp.concatenate([window, global_keys, random_keys], axis=3)
    key_list = all_keys[0].reshape(head_count, block_count, slot_total * block_rows, head_width)
    value_list = all_keys[1].reshape(head_count, block_count, slot_total * block_rows, head_width)
    block_range = jnp.arange(block_count, dtype=jnp.int32)
    left_valid = jnp.logical_not((block_range == 0) & (device == 0))
    right_valid = jnp.logical_not((block_range == block_count - 1) & (device == seq_count - 1))
    valid = jnp.concatenate(
        [
            left_valid[:, None],
            jnp.ones((block_count, 1), bool),
            right_valid[:, None],
            jnp.ones((block_count, global_count + slot_count), bool),
        ],
        1,
    )
    mask = jnp.repeat(valid, block_rows, axis=1)[None, :, None, :]
    query_blocks = queries.reshape(head_count, block_count, block_rows, head_width)
    grad_blocks = grad_out.reshape(head_count, block_count, block_rows, head_width)
    scores = (
        jnp.einsum("hnqd,hnkd->hnqk", query_blocks, key_list, preferred_element_type=jnp.float32)
        * score_scale
    )
    row_max = jnp.max(jnp.where(mask, scores, -1e30), -1)
    total = jnp.sum(jnp.where(mask, jnp.exp(scores - row_max[..., None]), 0.0), -1)
    log_total = row_max + jnp.log(total)
    probs = jnp.where(mask, jnp.exp(scores - log_total[..., None]), 0.0)
    probs_low = probs.astype(jnp.bfloat16)
    output = jnp.einsum(
        "hnqk,hnkd->hnqd", probs_low, value_list, preferred_element_type=jnp.float32
    )
    row_dot = jnp.sum(grad_blocks.astype(jnp.float32) * output, -1)
    grad_probs = jnp.einsum(
        "hnqd,hnkd->hnqk", grad_blocks, value_list, preferred_element_type=jnp.float32
    )
    scores_low = (probs * (grad_probs - row_dot[..., None])).astype(jnp.bfloat16)
    grad_query = score_scale * jnp.einsum(
        "hnqk,hnkd->hnqd", scores_low, key_list, preferred_element_type=jnp.float32
    )
    key_terms = score_scale * jnp.einsum(
        "hnqk,hnqd->hnkd", scores_low, query_blocks, preferred_element_type=jnp.float32
    )
    value_terms = jnp.einsum(
        "hnqk,hnqd->hnkd", probs_low, grad_blocks, preferred_element_type=jnp.float32
    )
    grads = jnp.stack([key_terms, value_terms]).reshape(
        2, head_count, block_count, slot_total, block_rows, head_width
    )
    no_pad = (0, 0)
    frame_sum = jnp.pad(grads[:, :, :, 0], (no_pad, no_pad, (0, 2), no_pad, no_pad))
    frame_sum = frame_sum + jnp.pad(grads[:, :, :, 1], (no_pad, no_pad, (1, 1), no_pad, no_pad))
    frame_sum = frame_sum + jnp.pad(grads[:, :, :, 2], (no_pad, no_pad, (2, 0), no_pad, no_pad))
    own_grads = frame_sum[:, :, 1 : block_count + 1]
    rim_parts = jnp.concatenate([frame_sum[:, :, 0], frame_sum[:, :, block_count + 1]], axis=2)
    rim_back = with_halo(rim_parts.astype(jnp.bfloat16), (("seq", 2),), block_rows).astype(
        rim_parts.dtype
    )
    own_grads = own_grads.at[:, :, 0].add(rim_back[:, :, 0:block_rows])
    own_grads = own_grads.at[:, :, block_count - 1].add(
        rim_back[:, :, 3 * block_rows : 4 * block_rows]
    )
    global_part = jnp.sum(grads[:, :, :, 3 : 3 + global_count], axis=2)
    global_total = lax.psum(global_part, "seq")
    global_onehot = (
        (global_local[:, None] == block_range[None, :]) & (global_owner == device)[:, None]
    ).astype(jnp.float32)
    own_grads = own_grads + jnp.einsum(
        "gn,chgbd->chnbd", global_onehot, global_total, precision=lax.Precision.HIGHEST
    )
    random_part = grads[:, :, :, 3 + global_count :]
    local_float = (random_local[..., None] == block_range).astype(jnp.float32)
    send_back = jnp.einsum(
        "hqjl,chqjbd->jchlbd", local_float, random_part, precision=lax.Precision.HIGHEST
    )
    send_back = send_back.astype(jnp.bfloat16).reshape(
        slot_count, 2, head_count, row_count, head_width
    )
    pieces = []
    for slot_index in range(slot_count):
        moving = send_back[slot_index]
        for bit_index in sections:
            arrived = swapped(moving, "seq", bit_index)
            flag_now = jnp.right_shift(xor_masks[:, slot_index], bit_index) & 1 == 1
            moving = jnp.where(flag_now[None, :, None, None], arrived, moving)
        pieces.append(moving)
    returned = jnp.stack(pieces)
    returned_sum = jnp.sum(returned.astype(jnp.float32), axis=0).reshape(
        2, head_count, block_count, block_rows, head_width
    )
    own_grads = own_grads + returned_sum
    grad_queries = grad_query.reshape(head_count, row_count, head_width).astype(jnp.bfloat16)
    grad_keys = own_grads[0].reshape(head_count, row_count, head_width).astype(jnp.bfloat16)
    grad_values = own_grads[1].reshape(head_count, row_count, head_width).astype(jnp.bfloat16)
    return (grad_queries, grad_keys, grad_values)


def on_device(queries, keys, values, grad_out, rand_ids, global_ids):
    count = lax.axis_size("seq")
    rows, width = queries.shape[1:]
    gathered_bytes = 4 * count * queries.size * queries.dtype.itemsize
    if gathered_bytes <= GATHER_BYTES and count % 2 == 0 and rows == width:
        return gathered(queries, keys, values, grad_out, rand_ids, global_ids)
    return routed(queries, keys, values, grad_out, rand_ids, global_ids)


def solution(mesh):
    in_specs = (
        P("head", "seq", None),
        P("head", "seq", None),
        P("head", "seq", None),
        P("head", "seq", None),
        P("head", "seq", None),
        P(),
    )
    out_specs = (P("head", "seq", None), P("head", "seq", None), P("head", "seq", None))
    return jax.shard_map(
        on_device, mesh=mesh, in_specs=in_specs, out_specs=out_specs, check_vma=False
    )
```

```python
import functools
import math

import jax
import jax.numpy as jnp
from jax import lax
from jax.experimental import pallas as pl
from jax.experimental.pallas import tpu as pltpu
from jax.sharding import PartitionSpec as P


GATHER_BYTES = 8 * 2**20
KERNEL_VMEM = 16 * 2**20
LOG2E = math.log2(math.e)
NEVER = -1e30
GROUP = 4
NT = (((1,), (1,)), ((), ()))


def pack_kernel(sizes, ids_hbm, gids_hbm, k_ref, v_ref, q_ref, g_ref, a_ref, b_ref, ids_ref, gids_ref, sems):
    heads, _, rows, _, block_rows, slots, _ = sizes
    blocks = rows // block_rows
    small = [
        pltpu.make_async_copy(ids_hbm, ids_ref, sems.at[0]),
        pltpu.make_async_copy(gids_hbm, gids_ref, sems.at[1]),
    ]
    copies = []
    for i, (src, dst, first) in enumerate(
        ((k_ref, a_ref, 0), (v_ref, a_ref, heads), (q_ref, b_ref, 0), (g_ref, b_ref, heads))
    ):
        for h in range(heads):
            copies.append(
                pltpu.make_async_copy(
                    src.at[h], dst.at[pl.ds((first + h) * rows, rows)], sems.at[2 + i * heads + h]
                )
            )
    for c in small + copies:
        c.start()
    head_rows = a_ref.shape[0] - 2 * heads * rows
    row = lax.broadcasted_iota(jnp.int32, (head_rows, rows), 0)
    lane = lax.broadcasted_iota(jnp.int32, (head_rows, rows), 1)
    me = lax.axis_index("seq")
    block = jnp.zeros_like(lane)
    for n in range(1, blocks):
        block = block + jnp.where(lane >= n * block_rows, 1, 0)
    tile = me * blocks + block
    for c in small:
        c.wait()
    for h in range(heads):
        for j in range(slots):
            ids = jnp.full_like(lane, ids_ref[h, 0, j])
            for n in range(1, blocks):
                ids = jnp.where(block == n, ids_ref[h, n, j], ids)
            tile = jnp.where(row == h * slots + j, ids, tile)
    for n in range(gids_ref.shape[0]):
        tile = jnp.where(row == heads * slots + 1 + n, gids_ref[n], tile)
    a_ref[2 * heads * rows :] = tile.astype(jnp.float32).astype(jnp.bfloat16)
    b_ref[2 * heads * rows :] = tile.astype(jnp.float32).astype(jnp.bfloat16)
    for c in copies:
        c.wait()


class Shards:
    def __init__(self, sizes, a_refs, b_refs):
        self.heads, self.count, self.rows, self.width, self.block_rows, self.slots, self.gids = sizes
        self.blocks = self.rows // self.block_rows
        self.a, self.b = a_refs, b_refs
        self.scale = 1.0 / math.sqrt(self.width)
        self.rate = self.scale * LOG2E
        self.key_heads = [self.head(x) for x in a_refs]
        self.query_heads = [self.head(x) for x in b_refs]

    def part(self, refs, index, group):
        found = [refs[s][index * self.rows : (index + 1) * self.rows] for s in group]
        return found[0] if len(found) == 1 else jnp.concatenate(found)

    def k(self, h, group):
        return self.part(self.a, h, group)

    def v(self, h, group):
        return self.part(self.a, self.heads + h, group)

    def q(self, h, group):
        return self.part(self.b, h, group)

    def g(self, h, group):
        return self.part(self.b, self.heads + h, group)

    def key_ids(self, group):
        height = len(group) * self.blocks
        row = lax.broadcasted_iota(jnp.int32, (height, self.rows), 0).astype(jnp.float32)
        base = self.heads * self.slots
        nk = jnp.zeros((height, self.rows), jnp.float32)
        for i, s in enumerate(group):
            first = self.key_heads[s][base : base + 1, 0:1] - i * self.blocks
            nk = jnp.where(row >= i * self.blocks, row + first, nk)
        seen = jnp.zeros((height, self.rows), jnp.float32)
        for n in range(self.gids):
            gid = self.key_heads[group[0]][base + 1 + n : base + 2 + n]
            seen = seen + jnp.where(nk == gid, 1.0, 0.0)
        return nk, seen

    def head(self, ref):
        return ref[2 * self.heads * self.rows :].astype(jnp.float32)

    def bias(self, keys, group):
        nk, seen = keys
        out = []
        for h in range(self.heads):
            cols = []
            for s in group:
                head = self.query_heads[s]
                nq = head[self.heads * self.slots :][:1]
                count = seen + jnp.where(jnp.abs(nk - nq) <= 1.0, 1.0, 0.0)
                for j in range(self.slots):
                    r = h * self.slots + j
                    count = count + jnp.where(nk == head[r : r + 1], 1.0, 0.0)
                cols.append(jnp.where(count > 0.5, jnp.log2(jnp.maximum(count, 1.0)), NEVER))
            out.append(cols[0] if len(cols) == 1 else jnp.concatenate(cols, axis=1))
        return out

    def scores(self, h, keys, queries):
        return (
            lax.dot_general(self.k(h, keys), self.q(h, queries), NT, preferred_element_type=jnp.float32),
            lax.dot_general(self.v(h, keys), self.g(h, queries), NT, preferred_element_type=jnp.float32),
        )

    def stats(self, scored, bias, keep):
        s, dp = scored
        lanes = s.shape[1]
        steps = self.block_rows // 8
        top = None
        for kb in range(bias.shape[0]):
            x = s[kb * self.block_rows : (kb + 1) * self.block_rows] * self.rate + bias[kb : kb + 1]
            x = jnp.max(x.reshape(steps, 8, lanes), axis=0)
            top = x if top is None else jnp.maximum(top, x)
        top = jnp.maximum(jnp.max(top, axis=0, keepdims=True), 0.5 * NEVER)
        acc_l = acc_d = None
        for kb in range(bias.shape[0]):
            cut = slice(kb * self.block_rows, (kb + 1) * self.block_rows)
            e = jnp.exp2(s[cut] * self.rate + (bias[kb : kb + 1] - top))
            keep(kb, cut, e, dp[cut])
            d = jnp.sum((e * dp[cut]).reshape(steps, 8, lanes), axis=0)
            e = jnp.sum(e.reshape(steps, 8, lanes), axis=0)
            acc_l = e if acc_l is None else acc_l + e
            acc_d = d if acc_d is None else acc_d + d
        return top, jnp.sum(acc_l, axis=0, keepdims=True), jnp.sum(acc_d, axis=0, keepdims=True)


def stats_kernel(sizes, widths, *refs):
    n_keys, n_queries = widths
    a_refs, b_refs = refs[:n_keys], refs[n_keys : n_keys + n_queries]
    stat, e_ref, dp_ref = refs[n_keys + n_queries :]
    sh = Shards(sizes, a_refs, b_refs)
    keys, queries = list(range(n_keys)), list(range(n_queries))
    bias = sh.bias(sh.key_ids(keys), queries)
    scored = [sh.scores(h, keys, queries) for h in range(sh.heads)]
    for h in range(sh.heads):

        def keep(kb, cut, e, dp):
            e_ref[h, cut] = e
            dp_ref[h, cut] = dp

        for i, x in enumerate(sh.stats(scored[h], bias[h], keep)):
            stat[3 * h + i : 3 * h + i + 1] = x


def partner_kernel(sizes, widths, *refs):
    heads, rows = sizes[0], sizes[2]
    n_keys, n_queries = widths
    a_refs, (stat, e_ref, dp_ref) = refs[:n_keys], refs[n_keys : n_keys + 3]
    outs = refs[n_keys + 3 :]
    sh = Shards(sizes, a_refs, ())
    tn = (((0,), (0,)), ((), ()))
    for s in range(1, n_queries):
        lanes = slice(s * rows, (s + 1) * rows)
        for h in range(heads):
            k = sh.k(h, list(range(n_keys)))
            local = local_dot(stat, h, lanes)
            low, e_low = [], []
            for r in range(0, n_keys * rows, sh.block_rows):
                e = e_ref[h, r : r + sh.block_rows, lanes]
                e_low.append(e.astype(jnp.bfloat16))
                low.append((e * (dp_ref[h, r : r + sh.block_rows, lanes] - local)).astype(jnp.bfloat16))
            for i, x in enumerate((low, e_low)):
                x = lax.dot_general(jnp.concatenate(x), k, tn, preferred_element_type=jnp.float32)
                outs[s - 1][(i * heads + h) * rows : (i * heads + h + 1) * rows] = x.astype(outs[s - 1].dtype)


def local_dot(stat, h, lanes):
    total = stat[3 * h + 1 : 3 * h + 2, lanes]
    return stat[3 * h + 2 : 3 * h + 3, lanes] / jnp.where(total > 0.0, total, 1.0)


def whole_stats(stats, rows, h, s):
    holders = range(len(stats))

    def part(i, p):
        return stats[p][3 * h + i : 3 * h + i + 1, (s ^ p) * rows : ((s ^ p) + 1) * rows]

    top = functools.reduce(jnp.maximum, [part(0, p) for p in holders])
    scales = [jnp.exp2(part(0, p) - top) for p in holders]
    total = sum(part(1, p) * w for p, w in zip(holders, scales))
    weighted = sum(part(2, p) * w for p, w in zip(holders, scales))
    return top + jnp.log2(total), weighted / total


def grads_kernel(sizes, widths, *refs):
    heads, rows = sizes[0], sizes[2]
    n_keys, n_queries = widths
    b_refs = refs[:n_queries]
    stats, (e_ref, dp_ref) = refs[n_queries : 2 * n_queries], refs[2 * n_queries : 2 * n_queries + 2]
    kv_out = refs[2 * n_queries + 2 :]
    sh = Shards(sizes, (), b_refs)
    queries = list(range(n_queries))
    for h in range(heads):
        whole = [whole_stats(stats, rows, h, s) for s in queries]
        shift, dots = (jnp.concatenate([x[i] for x in whole], axis=1) for i in range(2))
        w = jnp.exp2(stats[0][3 * h : 3 * h + 1] - shift)
        p_low, ds_low = [], []
        for r in range(0, n_keys * rows, sh.block_rows):
            cut = slice(r, r + sh.block_rows)
            p = e_ref[h, cut] * w
            p_low.append(p.astype(jnp.bfloat16))
            ds_low.append((p * (dp_ref[h, cut] - dots)).astype(jnp.bfloat16))
        dk = jnp.dot(jnp.concatenate(ds_low), sh.q(h, queries), preferred_element_type=jnp.float32) * sh.scale
        dv = jnp.dot(jnp.concatenate(p_low), sh.g(h, queries), preferred_element_type=jnp.float32)
        for m in range(n_keys):
            cut = slice(m * rows, (m + 1) * rows)
            kv_out[m][h * rows : (h + 1) * rows] = dk[cut].astype(kv_out[m].dtype)
            kv_out[m][(heads + h) * rows : (heads + h + 1) * rows] = dv[cut].astype(kv_out[m].dtype)


def queries_kernel(sizes, widths, *refs):
    heads, rows = sizes[0], sizes[2]
    n_keys, n_queries = widths
    a_refs, refs = refs[:n_keys], refs[n_keys:]
    stats, (e_ref, dp_ref), refs = refs[:n_queries], refs[n_queries : n_queries + 2], refs[n_queries + 2 :]
    sums, out = refs[: n_queries - 1], refs[-1]
    sh = Shards(sizes, a_refs, ())
    for h in range(heads):
        shift, dots = whole_stats(stats, rows, h, 0)
        w = jnp.exp2(stats[0][3 * h : 3 * h + 1, 0:rows] - shift)
        low = []
        for r in range(0, n_keys * rows, sh.block_rows):
            cut = slice(r, r + sh.block_rows)
            low.append(((e_ref[h, cut, 0:rows] * w) * (dp_ref[h, cut, 0:rows] - dots)).astype(jnp.bfloat16))
        dq = lax.dot_general(
            jnp.concatenate(low), sh.k(h, list(range(n_keys))), (((0,), (0,)), ((), ())),
            preferred_element_type=jnp.float32,
        )
        for p in range(1, n_queries):
            lanes = slice(p * rows, (p + 1) * rows)
            w = jnp.exp2(stats[p][3 * h : 3 * h + 1, lanes] - shift)
            moved = w * (local_dot(stats[p], h, lanes) - dots)
            w, moved = (jnp.broadcast_to(x, (rows, rows)).T for x in (w, moved))
            first = sums[p - 1][h * rows : (h + 1) * rows].astype(jnp.float32)
            second = sums[p - 1][(heads + h) * rows : (heads + h + 1) * rows].astype(jnp.float32)
            dq = dq + (first * w + second * moved)
        out[h] = (dq * sh.scale).astype(out.dtype)


def sum_kernel(sizes, n_keys, *refs):
    heads, rows = sizes[0], sizes[2]
    parts, outs, bufs, sems = refs[:n_keys], refs[n_keys : n_keys + 2], refs[n_keys + 2 : -1], refs[-1]
    copies = []
    for i in range(2):
        for h in range(heads):
            cut = slice((i * heads + h) * rows, (i * heads + h + 1) * rows)
            total = sum(p[cut].astype(jnp.float32) for p in parts)
            bufs[i][h] = total.astype(bufs[i].dtype)
        copies.append(pltpu.make_async_copy(bufs[i], outs[i], sems.at[i]))
        copies[-1].start()
    for c in copies:
        c.wait()


def near(arrays):
    return [pltpu.with_memory_space_constraint(x, pltpu.VMEM) for x in arrays]


def exchanged(value, mask):
    return lax.ppermute(value, "seq", [(i, i ^ mask) for i in range(lax.axis_size("seq"))])


def key_moves(n_keys):
    direct = [m for m in range(n_keys - 1, 0, -1) if m & (m - 1) == 0]
    relayed = [m for m in range(1, n_keys) if m not in direct]
    return [(m, m) for m in direct], [(m, m & -m) for m in relayed]


def gathered(queries, keys, values, grad_out, rand_ids, global_ids):
    heads, rows, width = queries.shape
    blocks, slots = rand_ids.shape[1:]
    count = lax.axis_size("seq")
    n_keys = min(GROUP, count)
    n_queries = count // n_keys
    widths = (n_keys, n_queries)
    sizes = (heads, count, rows, width, rows // blocks, slots, global_ids.shape[0])
    head_rows = -(-(heads * slots + 1 + global_ids.shape[0]) // 16) * 16
    vmem = pl.BlockSpec(memory_space=pltpu.VMEM)
    anyspace = pl.BlockSpec(memory_space=pl.ANY)
    params = pltpu.CompilerParams(vmem_limit_bytes=KERNEL_VMEM)
    a, b = pl.pallas_call(
        functools.partial(pack_kernel, sizes),
        out_shape=(pltpu.VMEM((2 * heads * rows + head_rows, width), queries.dtype),) * 2,
        in_specs=[anyspace] * 6,
        out_specs=(vmem, vmem),
        scratch_shapes=[
            pltpu.SMEM(rand_ids.shape, jnp.int32),
            pltpu.SMEM(global_ids.shape, jnp.int32),
            pltpu.SemaphoreType.DMA((2 + 4 * heads,)),
        ],
    )(rand_ids, global_ids, keys, values, queries, grad_out)

    b_all = [b] + [exchanged(b, s * n_keys) for s in range(1, n_queries)]
    a_all = {0: a}
    for moves in key_moves(n_keys):
        for m, last in moves:
            a_all[m] = exchanged(a_all[m - last], last)
    a_all = [a_all[m] for m in range(n_keys)]
    lanes = n_queries * rows
    stat_rows = -(-3 * heads // 8) * 8
    stat, e, dp = pl.pallas_call(
        functools.partial(stats_kernel, sizes, widths),
        out_shape=(pltpu.VMEM((stat_rows, lanes), jnp.float32),)
        + (pltpu.VMEM((heads, n_keys * rows, lanes), jnp.float32),) * 2,
        compiler_params=params,
        in_specs=[vmem] * count_of(widths),
        out_specs=(vmem,) * 3,
    )(*near(a_all), *near(b_all))
    stats = [stat] + [exchanged(stat, s * n_keys) for s in range(1, n_queries)]
    sums = pl.pallas_call(
        functools.partial(partner_kernel, sizes, widths),
        out_shape=(pltpu.VMEM((2 * heads * rows, width), queries.dtype),) * (n_queries - 1),
        compiler_params=params,
        in_specs=[vmem] * (n_keys + 3),
        out_specs=(vmem,) * (n_queries - 1),
    )(*near(a_all), *near([stat, e, dp]))
    sums = [exchanged(x, s * n_keys) for s, x in zip(range(1, n_queries), sums)]
    shapes = [pltpu.VMEM((2 * heads * rows, width), jnp.float32)]
    shapes += [pltpu.VMEM((2 * heads * rows, width), queries.dtype)] * (n_keys - 1)
    parts = pl.pallas_call(
        functools.partial(grads_kernel, sizes, widths),
        out_shape=tuple(shapes),
        compiler_params=params,
        in_specs=[vmem] * (2 * n_queries + 2),
        out_specs=(vmem,) * len(shapes),
    )(*near(b_all), *near(stats), *near([e, dp]))
    parts = [parts[0]] + [exchanged(parts[m], m) for m in range(1, n_keys)]
    out = jax.ShapeDtypeStruct(queries.shape, queries.dtype)
    grad_queries = pl.pallas_call(
        functools.partial(queries_kernel, sizes, widths),
        out_shape=out,
        compiler_params=params,
        in_specs=[vmem] * (n_keys + 2 * n_queries + 1),
        out_specs=vmem,
    )(*near(a_all), *near(stats), *near([e, dp]), *near(sums))
    buf = pltpu.VMEM(queries.shape, queries.dtype)
    grad_keys, grad_values = pl.pallas_call(
        functools.partial(sum_kernel, sizes, n_keys),
        out_shape=(out, out),
        compiler_params=params,
        in_specs=[vmem] * n_keys,
        out_specs=(anyspace,) * 2,
        scratch_shapes=[buf, buf, pltpu.SemaphoreType.DMA((2,))],
    )(*near(parts))
    return grad_queries, grad_keys, grad_values


def count_of(widths):
    return widths[0] + widths[1]


def with_halo(value, sides, width):
    for axis, dim in sides:
        peers, length = (lax.axis_size(axis), value.shape[dim])
        up = [(i, (i + 1) % peers) for i in range(peers - 1)]
        down = [(j, i) for i, j in up]
        last = lax.slice_in_dim(value, length - width, length, axis=dim)
        initial = lax.slice_in_dim(value, 0, width, axis=dim)
        before = lax.ppermute(last, axis, up)
        after = lax.ppermute(initial, axis, down)
        value = jnp.concatenate([before, value, after], axis=dim)
    return value


def swapped(value, axis, distance):
    mask = 2**distance
    pairs = [(source, source ^ mask) for source in range(lax.axis_size(axis))]
    return lax.ppermute(value, axis, pairs)


def section_list(section_count):
    return list(range(section_count))


def routed(queries, keys, values, grad_out, rand_ids, global_ids):
    head_count, row_count, head_width = queries.shape
    block_count = rand_ids.shape[1]
    slot_count = rand_ids.shape[2]
    block_rows = row_count // block_count
    global_count = global_ids.shape[0]
    slot_total = 3 + global_count + slot_count
    device = lax.axis_index("seq")
    seq_count = lax.axis_size("seq")
    sections = section_list(seq_count.bit_length() - 1)
    score_scale = 1.0 / math.sqrt(head_width)
    key_vals = jnp.stack([keys, values])
    padded = with_halo(key_vals, (("seq", 2),), block_rows)
    padded_blocks = padded.reshape(2, head_count, block_count + 2, block_rows, head_width)
    window = jnp.stack(
        [
            padded_blocks[:, :, 0:block_count],
            padded_blocks[:, :, 1 : block_count + 1],
            padded_blocks[:, :, 2 : block_count + 2],
        ],
        3,
    )
    key_blocks = key_vals.reshape(2, head_count, block_count, block_rows, head_width)
    global_local = global_ids % block_count
    global_owner = global_ids // block_count
    owned = (global_owner == device).astype(jnp.float32)
    picked = jnp.take(key_blocks, global_local, axis=2).astype(jnp.float32)
    global_sum = lax.psum(picked * owned[None, None, :, None, None], "seq")
    global_kv = global_sum.astype(jnp.bfloat16)
    global_keys = jnp.broadcast_to(
        global_kv[:, :, None], (2, head_count, block_count, global_count, block_rows, head_width)
    )
    xor_masks = jnp.bitwise_xor(rand_ids[:, 0, :] // block_count, device)
    pieces = []
    for slot_index in range(slot_count):
        moving = key_vals
        for bit_index in sections:
            arrived = swapped(moving, "seq", bit_index)
            flag_now = jnp.right_shift(xor_masks[:, slot_index], bit_index) & 1 == 1
            moving = jnp.where(flag_now[None, :, None, None], arrived, moving)
        pieces.append(moving)
    routed = jnp.stack(pieces)
    routed_blocks = routed.reshape(slot_count, 2, head_count, block_count, block_rows, head_width)
    random_local = rand_ids % block_count
    local_onehot = (random_local[..., None] == jnp.arange(block_count, dtype=jnp.int32)).astype(
        jnp.bfloat16
    )
    random_keys = jnp.einsum(
        "hqjl,jchlbd->chqjbd", local_onehot, routed_blocks, preferred_element_type=jnp.float32
    ).astype(jnp.bfloat16)
    all_keys = jnp.concatenate([window, global_keys, random_keys], axis=3)
    key_list = all_keys[0].reshape(head_count, block_count, slot_total * block_rows, head_width)
    value_list = all_keys[1].reshape(head_count, block_count, slot_total * block_rows, head_width)
    block_range = jnp.arange(block_count, dtype=jnp.int32)
    left_valid = jnp.logical_not((block_range == 0) & (device == 0))
    right_valid = jnp.logical_not((block_range == block_count - 1) & (device == seq_count - 1))
    valid = jnp.concatenate(
        [
            left_valid[:, None],
            jnp.ones((block_count, 1), bool),
            right_valid[:, None],
            jnp.ones((block_count, global_count + slot_count), bool),
        ],
        1,
    )
    mask = jnp.repeat(valid, block_rows, axis=1)[None, :, None, :]
    query_blocks = queries.reshape(head_count, block_count, block_rows, head_width)
    grad_blocks = grad_out.reshape(head_count, block_count, block_rows, head_width)
    scores = (
        jnp.einsum("hnqd,hnkd->hnqk", query_blocks, key_list, preferred_element_type=jnp.float32)
        * score_scale
    )
    row_max = jnp.max(jnp.where(mask, scores, -1e30), -1)
    total = jnp.sum(jnp.where(mask, jnp.exp(scores - row_max[..., None]), 0.0), -1)
    log_total = row_max + jnp.log(total)
    probs = jnp.where(mask, jnp.exp(scores - log_total[..., None]), 0.0)
    probs_low = probs.astype(jnp.bfloat16)
    output = jnp.einsum(
        "hnqk,hnkd->hnqd", probs_low, value_list, preferred_element_type=jnp.float32
    )
    row_dot = jnp.sum(grad_blocks.astype(jnp.float32) * output, -1)
    grad_probs = jnp.einsum(
        "hnqd,hnkd->hnqk", grad_blocks, value_list, preferred_element_type=jnp.float32
    )
    scores_low = (probs * (grad_probs - row_dot[..., None])).astype(jnp.bfloat16)
    grad_query = score_scale * jnp.einsum(
        "hnqk,hnkd->hnqd", scores_low, key_list, preferred_element_type=jnp.float32
    )
    key_terms = score_scale * jnp.einsum(
        "hnqk,hnqd->hnkd", scores_low, query_blocks, preferred_element_type=jnp.float32
    )
    value_terms = jnp.einsum(
        "hnqk,hnqd->hnkd", probs_low, grad_blocks, preferred_element_type=jnp.float32
    )
    grads = jnp.stack([key_terms, value_terms]).reshape(
        2, head_count, block_count, slot_total, block_rows, head_width
    )
    no_pad = (0, 0)
    frame_sum = jnp.pad(grads[:, :, :, 0], (no_pad, no_pad, (0, 2), no_pad, no_pad))
    frame_sum = frame_sum + jnp.pad(grads[:, :, :, 1], (no_pad, no_pad, (1, 1), no_pad, no_pad))
    frame_sum = frame_sum + jnp.pad(grads[:, :, :, 2], (no_pad, no_pad, (2, 0), no_pad, no_pad))
    own_grads = frame_sum[:, :, 1 : block_count + 1]
    rim_parts = jnp.concatenate([frame_sum[:, :, 0], frame_sum[:, :, block_count + 1]], axis=2)
    rim_back = with_halo(rim_parts.astype(jnp.bfloat16), (("seq", 2),), block_rows).astype(
        rim_parts.dtype
    )
    own_grads = own_grads.at[:, :, 0].add(rim_back[:, :, 0:block_rows])
    own_grads = own_grads.at[:, :, block_count - 1].add(
        rim_back[:, :, 3 * block_rows : 4 * block_rows]
    )
    global_part = jnp.sum(grads[:, :, :, 3 : 3 + global_count], axis=2)
    global_total = lax.psum(global_part, "seq")
    global_onehot = (
        (global_local[:, None] == block_range[None, :]) & (global_owner == device)[:, None]
    ).astype(jnp.float32)
    own_grads = own_grads + jnp.einsum(
        "gn,chgbd->chnbd", global_onehot, global_total, precision=lax.Precision.HIGHEST
    )
    random_part = grads[:, :, :, 3 + global_count :]
    local_float = (random_local[..., None] == block_range).astype(jnp.float32)
    send_back = jnp.einsum(
        "hqjl,chqjbd->jchlbd", local_float, random_part, precision=lax.Precision.HIGHEST
    )
    send_back = send_back.astype(jnp.bfloat16).reshape(
        slot_count, 2, head_count, row_count, head_width
    )
    pieces = []
    for slot_index in range(slot_count):
        moving = send_back[slot_index]
        for bit_index in sections:
            arrived = swapped(moving, "seq", bit_index)
            flag_now = jnp.right_shift(xor_masks[:, slot_index], bit_index) & 1 == 1
            moving = jnp.where(flag_now[None, :, None, None], arrived, moving)
        pieces.append(moving)
    returned = jnp.stack(pieces)
    returned_sum = jnp.sum(returned.astype(jnp.float32), axis=0).reshape(
        2, head_count, block_count, block_rows, head_width
    )
    own_grads = own_grads + returned_sum
    grad_queries = grad_query.reshape(head_count, row_count, head_width).astype(jnp.bfloat16)
    grad_keys = own_grads[0].reshape(head_count, row_count, head_width).astype(jnp.bfloat16)
    grad_values = own_grads[1].reshape(head_count, row_count, head_width).astype(jnp.bfloat16)
    return (grad_queries, grad_keys, grad_values)


def on_device(queries, keys, values, grad_out, rand_ids, global_ids):
    count = lax.axis_size("seq")
    rows, width = queries.shape[1:]
    gathered_bytes = 4 * count * queries.size * queries.dtype.itemsize
    if gathered_bytes <= GATHER_BYTES and count & (count - 1) == 0 and rows == width:
        return gathered(queries, keys, values, grad_out, rand_ids, global_ids)
    return routed(queries, keys, values, grad_out, rand_ids, global_ids)


def solution(mesh):
    in_specs = (
        P("head", "seq", None),
        P("head", "seq", None),
        P("head", "seq", None),
        P("head", "seq", None),
        P("head", "seq", None),
        P(),
    )
    out_specs = (P("head", "seq", None), P("head", "seq", None), P("head", "seq", None))
    return jax.shard_map(
        on_device, mesh=mesh, in_specs=in_specs, out_specs=out_specs, check_vma=False
    )
```

```python
import functools
import math

import jax
import jax.numpy as jnp
from jax import lax
from jax.experimental import pallas as pl
from jax.experimental.pallas import tpu as pltpu
from jax.sharding import PartitionSpec as P


GATHER_BYTES = 8 * 2**20
KERNEL_VMEM = 16 * 2**20
LOG2E = math.log2(math.e)
NEVER = -1e30
GROUP = 4
NT = (((1,), (1,)), ((), ()))


def pack_kernel(sizes, ids_hbm, gids_hbm, k_ref, v_ref, q_ref, g_ref, a_ref, b_ref, ids_ref, gids_ref, sems):
    heads, _, rows, _, block_rows, slots, _ = sizes
    blocks = rows // block_rows
    small = [
        pltpu.make_async_copy(ids_hbm, ids_ref, sems.at[0]),
        pltpu.make_async_copy(gids_hbm, gids_ref, sems.at[1]),
    ]
    copies = []
    for i, (src, dst, first) in enumerate(
        ((k_ref, a_ref, 0), (v_ref, a_ref, heads), (q_ref, b_ref, 0), (g_ref, b_ref, heads))
    ):
        for h in range(heads):
            copies.append(
                pltpu.make_async_copy(
                    src.at[h], dst.at[pl.ds((first + h) * rows, rows)], sems.at[2 + i * heads + h]
                )
            )
    for c in small + copies:
        c.start()
    head_rows = a_ref.shape[0] - 2 * heads * rows
    row = lax.broadcasted_iota(jnp.int32, (head_rows, rows), 0)
    lane = lax.broadcasted_iota(jnp.int32, (head_rows, rows), 1)
    me = lax.axis_index("seq")
    block = jnp.zeros_like(lane)
    for n in range(1, blocks):
        block = block + jnp.where(lane >= n * block_rows, 1, 0)
    tile = me * blocks + block
    for c in small:
        c.wait()
    for h in range(heads):
        for j in range(slots):
            ids = jnp.full_like(lane, ids_ref[h, 0, j])
            for n in range(1, blocks):
                ids = jnp.where(block == n, ids_ref[h, n, j], ids)
            tile = jnp.where(row == h * slots + j, ids, tile)
    for n in range(gids_ref.shape[0]):
        tile = jnp.where(row == heads * slots + 1 + n, gids_ref[n], tile)
    a_ref[2 * heads * rows :] = tile.astype(jnp.float32).astype(jnp.bfloat16)
    b_ref[2 * heads * rows :] = tile.astype(jnp.float32).astype(jnp.bfloat16)
    for c in copies:
        c.wait()


class Shards:
    def __init__(self, sizes, a_refs, b_refs):
        self.heads, self.count, self.rows, self.width, self.block_rows, self.slots, self.gids = sizes
        self.blocks = self.rows // self.block_rows
        self.a, self.b = a_refs, b_refs
        self.scale = 1.0 / math.sqrt(self.width)
        self.rate = self.scale * LOG2E
        self.key_heads = [self.head(x) for x in a_refs]
        self.query_heads = [self.head(x) for x in b_refs]

    def part(self, refs, index, group):
        found = [refs[s][index * self.rows : (index + 1) * self.rows] for s in group]
        return found[0] if len(found) == 1 else jnp.concatenate(found)

    def k(self, h, group):
        return self.part(self.a, h, group)

    def v(self, h, group):
        return self.part(self.a, self.heads + h, group)

    def q(self, h, group):
        return self.part(self.b, h, group)

    def g(self, h, group):
        return self.part(self.b, self.heads + h, group)

    def key_ids(self, group):
        height = len(group) * self.blocks
        row = lax.broadcasted_iota(jnp.int32, (height, self.rows), 0).astype(jnp.float32)
        base = self.heads * self.slots
        nk = jnp.zeros((height, self.rows), jnp.float32)
        for i, s in enumerate(group):
            first = self.key_heads[s][base : base + 1, 0:1] - i * self.blocks
            nk = jnp.where(row >= i * self.blocks, row + first, nk)
        seen = jnp.zeros((height, self.rows), jnp.float32)
        for n in range(self.gids):
            gid = self.key_heads[group[0]][base + 1 + n : base + 2 + n]
            seen = seen + jnp.where(nk == gid, 1.0, 0.0)
        return nk, seen

    def head(self, ref):
        return ref[2 * self.heads * self.rows :].astype(jnp.float32)

    def bias(self, keys, group):
        nk, seen = keys
        out = []
        for h in range(self.heads):
            cols = []
            for s in group:
                head = self.query_heads[s]
                nq = head[self.heads * self.slots :][:1]
                count = seen + jnp.where(jnp.abs(nk - nq) <= 1.0, 1.0, 0.0)
                for j in range(self.slots):
                    r = h * self.slots + j
                    count = count + jnp.where(nk == head[r : r + 1], 1.0, 0.0)
                cols.append(jnp.where(count > 0.5, jnp.log2(jnp.maximum(count, 1.0)), NEVER))
            out.append(cols[0] if len(cols) == 1 else jnp.concatenate(cols, axis=1))
        return out

    def scores(self, h, keys, queries):
        return (
            lax.dot_general(self.k(h, keys), self.q(h, queries), NT, preferred_element_type=jnp.float32),
            lax.dot_general(self.v(h, keys), self.g(h, queries), NT, preferred_element_type=jnp.float32),
        )

    def stats(self, scored, bias, keep, start=None):
        s, dp = scored
        lanes = s.shape[1]
        steps = self.block_rows // 8
        top = None
        for kb in range(bias.shape[0]):
            x = s[kb * self.block_rows : (kb + 1) * self.block_rows] * self.rate + bias[kb : kb + 1]
            x = jnp.max(x.reshape(steps, 8, lanes), axis=0)
            top = x if top is None else jnp.maximum(top, x)
        top = jnp.maximum(jnp.max(top, axis=0, keepdims=True), 0.5 * NEVER)
        if start:
            top = jnp.maximum(top, start[0])
        acc_l = acc_d = None
        for kb in range(bias.shape[0]):
            cut = slice(kb * self.block_rows, (kb + 1) * self.block_rows)
            e = jnp.exp2(s[cut] * self.rate + (bias[kb : kb + 1] - top))
            keep(kb, cut, e, dp[cut])
            d = jnp.sum((e * dp[cut]).reshape(steps, 8, lanes), axis=0)
            e = jnp.sum(e.reshape(steps, 8, lanes), axis=0)
            acc_l = e if acc_l is None else acc_l + e
            acc_d = d if acc_d is None else acc_d + d
        acc_l, acc_d = (jnp.sum(x, axis=0, keepdims=True) for x in (acc_l, acc_d))
        if start:
            w = jnp.exp2(start[0] - top)
            acc_l, acc_d = acc_l + start[1] * w, acc_d + start[2] * w
        return top, acc_l, acc_d


def stats_kernel(sizes, n_keys, n_queries, *refs):
    a_refs, b_refs = refs[:n_keys], refs[n_keys : n_keys + n_queries]
    before = refs[n_keys + n_queries : -3]
    stat, e_ref, dp_ref = refs[-3:]
    sh = Shards(sizes, a_refs, b_refs)
    keys, queries = list(range(n_keys)), list(range(n_queries))
    bias = sh.bias(sh.key_ids(keys), queries)
    scored = [sh.scores(h, keys, queries) for h in range(sh.heads)]
    for h in range(sh.heads):

        def keep(kb, cut, e, dp):
            e_ref[h, cut] = e
            dp_ref[h, cut] = dp

        start = [before[0][3 * h + i : 3 * h + i + 1] for i in range(3)] if before else None
        for i, x in enumerate(sh.stats(scored[h], bias[h], keep, start)):
            stat[3 * h + i : 3 * h + i + 1] = x


def kept_tiles(sh, kept, stat, h, lanes, shift=None):
    first, e_first, dp_first, e_last, dp_last = kept
    row = slice(3 * h, 3 * h + 1)
    top = stat[row, lanes]
    base = top if shift is None else shift
    for before, e_ref, dp_ref in ((first[row, lanes], e_first, dp_first), (top, e_last, dp_last)):
        w = None if before is base else jnp.exp2(before - base)
        for r in range(0, e_ref.shape[1], sh.block_rows):
            cut = slice(r, r + sh.block_rows)
            e = e_ref[h, cut, lanes]
            yield (e if w is None else e * w), dp_ref[h, cut, lanes]


def partner_kernel(sizes, widths, *refs):
    heads, rows = sizes[0], sizes[2]
    n_keys, n_queries = widths
    a_refs, stat, kept = refs[:n_keys], refs[n_keys], refs[n_keys + 1 : n_keys + 6]
    outs = refs[n_keys + 6 :]
    sh = Shards(sizes, a_refs, ())
    tn = (((0,), (0,)), ((), ()))
    for s in range(1, n_queries):
        lanes = slice(s * rows, (s + 1) * rows)
        for h in range(heads):
            k = sh.k(h, list(range(n_keys)))
            local = local_dot(stat, h, lanes)
            low, e_low = [], []
            for e, dp in kept_tiles(sh, kept, stat, h, lanes):
                e_low.append(e.astype(jnp.bfloat16))
                low.append((e * (dp - local)).astype(jnp.bfloat16))
            for i, x in enumerate((low, e_low)):
                x = lax.dot_general(jnp.concatenate(x), k, tn, preferred_element_type=jnp.float32)
                outs[s - 1][(i * heads + h) * rows : (i * heads + h + 1) * rows] = x.astype(outs[s - 1].dtype)


def local_dot(stat, h, lanes):
    total = stat[3 * h + 1 : 3 * h + 2, lanes]
    return stat[3 * h + 2 : 3 * h + 3, lanes] / jnp.where(total > 0.0, total, 1.0)


def whole_stats(stats, rows, h, s):
    holders = range(len(stats))

    def part(i, p):
        return stats[p][3 * h + i : 3 * h + i + 1, (s ^ p) * rows : ((s ^ p) + 1) * rows]

    top = functools.reduce(jnp.maximum, [part(0, p) for p in holders])
    scales = [jnp.exp2(part(0, p) - top) for p in holders]
    total = sum(part(1, p) * w for p, w in zip(holders, scales))
    weighted = sum(part(2, p) * w for p, w in zip(holders, scales))
    return top + jnp.log2(total), weighted / total


def grads_kernel(sizes, widths, *refs):
    heads, rows = sizes[0], sizes[2]
    n_keys, n_queries = widths
    b_refs = refs[:n_queries]
    stats, kept = refs[n_queries : 2 * n_queries], refs[2 * n_queries : 2 * n_queries + 5]
    kv_out = refs[2 * n_queries + 5 :]
    sh = Shards(sizes, (), b_refs)
    queries = list(range(n_queries))
    for h in range(heads):
        whole = [whole_stats(stats, rows, h, s) for s in queries]
        shift, dots = (jnp.concatenate([x[i] for x in whole], axis=1) for i in range(2))
        p_low, ds_low = [], []
        for p, dp in kept_tiles(sh, kept, stats[0], h, slice(0, n_queries * rows), shift):
            p_low.append(p.astype(jnp.bfloat16))
            ds_low.append((p * (dp - dots)).astype(jnp.bfloat16))
        dk = jnp.dot(jnp.concatenate(ds_low), sh.q(h, queries), preferred_element_type=jnp.float32) * sh.scale
        dv = jnp.dot(jnp.concatenate(p_low), sh.g(h, queries), preferred_element_type=jnp.float32)
        for m in range(n_keys):
            cut = slice(m * rows, (m + 1) * rows)
            kv_out[m][h * rows : (h + 1) * rows] = dk[cut].astype(kv_out[m].dtype)
            kv_out[m][(heads + h) * rows : (heads + h + 1) * rows] = dv[cut].astype(kv_out[m].dtype)


def queries_kernel(sizes, widths, *refs):
    heads, rows = sizes[0], sizes[2]
    n_keys, n_queries = widths
    a_refs, refs = refs[:n_keys], refs[n_keys:]
    stats, kept, refs = refs[:n_queries], refs[n_queries : n_queries + 5], refs[n_queries + 5 :]
    sums, out = refs[: n_queries - 1], refs[-1]
    sh = Shards(sizes, a_refs, ())
    for h in range(heads):
        shift, dots = whole_stats(stats, rows, h, 0)
        low = []
        for p, dp in kept_tiles(sh, kept, stats[0], h, slice(0, rows), shift):
            low.append((p * (dp - dots)).astype(jnp.bfloat16))
        dq = lax.dot_general(
            jnp.concatenate(low), sh.k(h, list(range(n_keys))), (((0,), (0,)), ((), ())),
            preferred_element_type=jnp.float32,
        )
        for p in range(1, n_queries):
            lanes = slice(p * rows, (p + 1) * rows)
            w = jnp.exp2(stats[p][3 * h : 3 * h + 1, lanes] - shift)
            moved = w * (local_dot(stats[p], h, lanes) - dots)
            w, moved = (jnp.broadcast_to(x, (rows, rows)).T for x in (w, moved))
            first = sums[p - 1][h * rows : (h + 1) * rows].astype(jnp.float32)
            second = sums[p - 1][(heads + h) * rows : (heads + h + 1) * rows].astype(jnp.float32)
            dq = dq + (first * w + second * moved)
        out[h] = (dq * sh.scale).astype(out.dtype)


def sum_kernel(sizes, n_keys, *refs):
    heads, rows = sizes[0], sizes[2]
    parts, outs, bufs, sems = refs[:n_keys], refs[n_keys : n_keys + 2], refs[n_keys + 2 : -1], refs[-1]
    copies = []
    for i in range(2):
        for h in range(heads):
            cut = slice((i * heads + h) * rows, (i * heads + h + 1) * rows)
            total = sum(p[cut].astype(jnp.float32) for p in parts)
            bufs[i][h] = total.astype(bufs[i].dtype)
        copies.append(pltpu.make_async_copy(bufs[i], outs[i], sems.at[i]))
        copies[-1].start()
    for c in copies:
        c.wait()


def near(arrays):
    return [pltpu.with_memory_space_constraint(x, pltpu.VMEM) for x in arrays]


def exchanged(value, mask):
    return lax.ppermute(value, "seq", [(i, i ^ mask) for i in range(lax.axis_size("seq"))])


def key_moves(n_keys):
    direct = [m for m in range(n_keys - 1, 0, -1) if m & (m - 1) == 0]
    relayed = [m for m in range(1, n_keys) if m not in direct]
    return [(m, m) for m in direct], [(m, m & -m) for m in relayed]


def gathered(queries, keys, values, grad_out, rand_ids, global_ids):
    heads, rows, width = queries.shape
    blocks, slots = rand_ids.shape[1:]
    count = lax.axis_size("seq")
    n_keys = min(GROUP, count)
    n_queries = count // n_keys
    widths = (n_keys, n_queries)
    sizes = (heads, count, rows, width, rows // blocks, slots, global_ids.shape[0])
    head_rows = -(-(heads * slots + 1 + global_ids.shape[0]) // 16) * 16
    vmem = pl.BlockSpec(memory_space=pltpu.VMEM)
    anyspace = pl.BlockSpec(memory_space=pl.ANY)
    params = pltpu.CompilerParams(vmem_limit_bytes=KERNEL_VMEM)
    a, b = pl.pallas_call(
        functools.partial(pack_kernel, sizes),
        out_shape=(pltpu.VMEM((2 * heads * rows + head_rows, width), queries.dtype),) * 2,
        in_specs=[anyspace] * 6,
        out_specs=(vmem, vmem),
        scratch_shapes=[
            pltpu.SMEM(rand_ids.shape, jnp.int32),
            pltpu.SMEM(global_ids.shape, jnp.int32),
            pltpu.SemaphoreType.DMA((2 + 4 * heads,)),
        ],
    )(rand_ids, global_ids, keys, values, queries, grad_out)

    b_all = [b] + [exchanged(b, s * n_keys) for s in range(1, n_queries)]
    a_all = {0: a}
    for moves in key_moves(n_keys):
        for m, last in moves:
            a_all[m] = exchanged(a_all[m - last], last)
    a_all = [a_all[m] for m in range(n_keys)]
    lanes = n_queries * rows
    stat_rows = -(-3 * heads // 8) * 8
    a_all = near([a_all[0]] + [a_all[m] for moves in key_moves(n_keys) for m in sorted(m for m, _ in moves)])
    b_all = near(b_all)
    n_first = 1 + len(key_moves(n_keys)[0])
    stat, kept = None, []
    for part in (a_all[:n_first], a_all[n_first:]):
        before = near([stat]) if kept else []
        stat, e, dp = pl.pallas_call(
            functools.partial(stats_kernel, sizes, len(part), n_queries),
            out_shape=(pltpu.VMEM((stat_rows, lanes), jnp.float32),)
            + (pltpu.VMEM((heads, len(part) * rows, lanes), jnp.float32),) * 2,
            compiler_params=params,
            in_specs=[vmem] * (len(part) + n_queries + len(before)),
            out_specs=(vmem,) * 3,
        )(*part, *b_all, *before)
        kept += ([] if kept else [stat]) + [e, dp]
    kept = near(kept)
    stats = [stat] + [exchanged(stat, s * n_keys) for s in range(1, n_queries)]
    sums = pl.pallas_call(
        functools.partial(partner_kernel, sizes, widths),
        out_shape=(pltpu.VMEM((2 * heads * rows, width), queries.dtype),) * (n_queries - 1),
        compiler_params=params,
        in_specs=[vmem] * (n_keys + 6),
        out_specs=(vmem,) * (n_queries - 1),
    )(*a_all, *near([stat]), *kept)
    sums = [exchanged(x, s * n_keys) for s, x in zip(range(1, n_queries), sums)]
    shapes = [pltpu.VMEM((2 * heads * rows, width), jnp.float32)]
    shapes += [pltpu.VMEM((2 * heads * rows, width), queries.dtype)] * (n_keys - 1)
    parts = pl.pallas_call(
        functools.partial(grads_kernel, sizes, widths),
        out_shape=tuple(shapes),
        compiler_params=params,
        in_specs=[vmem] * (2 * n_queries + 5),
        out_specs=(vmem,) * len(shapes),
    )(*b_all, *near(stats), *kept)
    order = [m for moves in key_moves(n_keys) for m in sorted(m for m, _ in moves)]
    parts = [parts[0]] + [exchanged(x, m) for m, x in zip(order, parts[1:])]
    out = jax.ShapeDtypeStruct(queries.shape, queries.dtype)
    grad_queries = pl.pallas_call(
        functools.partial(queries_kernel, sizes, widths),
        out_shape=out,
        compiler_params=params,
        in_specs=[vmem] * (n_keys + 2 * n_queries + 4),
        out_specs=vmem,
    )(*a_all, *near(stats), *kept, *near(sums))
    buf = pltpu.VMEM(queries.shape, queries.dtype)
    grad_keys, grad_values = pl.pallas_call(
        functools.partial(sum_kernel, sizes, n_keys),
        out_shape=(out, out),
        compiler_params=params,
        in_specs=[vmem] * n_keys,
        out_specs=(anyspace,) * 2,
        scratch_shapes=[buf, buf, pltpu.SemaphoreType.DMA((2,))],
    )(*near(parts))
    return grad_queries, grad_keys, grad_values


def with_halo(value, sides, width):
    for axis, dim in sides:
        peers, length = (lax.axis_size(axis), value.shape[dim])
        up = [(i, (i + 1) % peers) for i in range(peers - 1)]
        down = [(j, i) for i, j in up]
        last = lax.slice_in_dim(value, length - width, length, axis=dim)
        initial = lax.slice_in_dim(value, 0, width, axis=dim)
        before = lax.ppermute(last, axis, up)
        after = lax.ppermute(initial, axis, down)
        value = jnp.concatenate([before, value, after], axis=dim)
    return value


def swapped(value, axis, distance):
    mask = 2**distance
    pairs = [(source, source ^ mask) for source in range(lax.axis_size(axis))]
    return lax.ppermute(value, axis, pairs)


def section_list(section_count):
    return list(range(section_count))


def routed(queries, keys, values, grad_out, rand_ids, global_ids):
    head_count, row_count, head_width = queries.shape
    block_count = rand_ids.shape[1]
    slot_count = rand_ids.shape[2]
    block_rows = row_count // block_count
    global_count = global_ids.shape[0]
    slot_total = 3 + global_count + slot_count
    device = lax.axis_index("seq")
    seq_count = lax.axis_size("seq")
    sections = section_list(seq_count.bit_length() - 1)
    score_scale = 1.0 / math.sqrt(head_width)
    key_vals = jnp.stack([keys, values])
    padded = with_halo(key_vals, (("seq", 2),), block_rows)
    padded_blocks = padded.reshape(2, head_count, block_count + 2, block_rows, head_width)
    window = jnp.stack(
        [
            padded_blocks[:, :, 0:block_count],
            padded_blocks[:, :, 1 : block_count + 1],
            padded_blocks[:, :, 2 : block_count + 2],
        ],
        3,
    )
    key_blocks = key_vals.reshape(2, head_count, block_count, block_rows, head_width)
    global_local = global_ids % block_count
    global_owner = global_ids // block_count
    owned = (global_owner == device).astype(jnp.float32)
    picked = jnp.take(key_blocks, global_local, axis=2).astype(jnp.float32)
    global_sum = lax.psum(picked * owned[None, None, :, None, None], "seq")
    global_kv = global_sum.astype(jnp.bfloat16)
    global_keys = jnp.broadcast_to(
        global_kv[:, :, None], (2, head_count, block_count, global_count, block_rows, head_width)
    )
    xor_masks = jnp.bitwise_xor(rand_ids[:, 0, :] // block_count, device)
    pieces = []
    for slot_index in range(slot_count):
        moving = key_vals
        for bit_index in sections:
            arrived = swapped(moving, "seq", bit_index)
            flag_now = jnp.right_shift(xor_masks[:, slot_index], bit_index) & 1 == 1
            moving = jnp.where(flag_now[None, :, None, None], arrived, moving)
        pieces.append(moving)
    routed = jnp.stack(pieces)
    routed_blocks = routed.reshape(slot_count, 2, head_count, block_count, block_rows, head_width)
    random_local = rand_ids % block_count
    local_onehot = (random_local[..., None] == jnp.arange(block_count, dtype=jnp.int32)).astype(
        jnp.bfloat16
    )
    random_keys = jnp.einsum(
        "hqjl,jchlbd->chqjbd", local_onehot, routed_blocks, preferred_element_type=jnp.float32
    ).astype(jnp.bfloat16)
    all_keys = jnp.concatenate([window, global_keys, random_keys], axis=3)
    key_list = all_keys[0].reshape(head_count, block_count, slot_total * block_rows, head_width)
    value_list = all_keys[1].reshape(head_count, block_count, slot_total * block_rows, head_width)
    block_range = jnp.arange(block_count, dtype=jnp.int32)
    left_valid = jnp.logical_not((block_range == 0) & (device == 0))
    right_valid = jnp.logical_not((block_range == block_count - 1) & (device == seq_count - 1))
    valid = jnp.concatenate(
        [
            left_valid[:, None],
            jnp.ones((block_count, 1), bool),
            right_valid[:, None],
            jnp.ones((block_count, global_count + slot_count), bool),
        ],
        1,
    )
    mask = jnp.repeat(valid, block_rows, axis=1)[None, :, None, :]
    query_blocks = queries.reshape(head_count, block_count, block_rows, head_width)
    grad_blocks = grad_out.reshape(head_count, block_count, block_rows, head_width)
    scores = (
        jnp.einsum("hnqd,hnkd->hnqk", query_blocks, key_list, preferred_element_type=jnp.float32)
        * score_scale
    )
    row_max = jnp.max(jnp.where(mask, scores, -1e30), -1)
    total = jnp.sum(jnp.where(mask, jnp.exp(scores - row_max[..., None]), 0.0), -1)
    log_total = row_max + jnp.log(total)
    probs = jnp.where(mask, jnp.exp(scores - log_total[..., None]), 0.0)
    probs_low = probs.astype(jnp.bfloat16)
    output = jnp.einsum(
        "hnqk,hnkd->hnqd", probs_low, value_list, preferred_element_type=jnp.float32
    )
    row_dot = jnp.sum(grad_blocks.astype(jnp.float32) * output, -1)
    grad_probs = jnp.einsum(
        "hnqd,hnkd->hnqk", grad_blocks, value_list, preferred_element_type=jnp.float32
    )
    scores_low = (probs * (grad_probs - row_dot[..., None])).astype(jnp.bfloat16)
    grad_query = score_scale * jnp.einsum(
        "hnqk,hnkd->hnqd", scores_low, key_list, preferred_element_type=jnp.float32
    )
    key_terms = score_scale * jnp.einsum(
        "hnqk,hnqd->hnkd", scores_low, query_blocks, preferred_element_type=jnp.float32
    )
    value_terms = jnp.einsum(
        "hnqk,hnqd->hnkd", probs_low, grad_blocks, preferred_element_type=jnp.float32
    )
    grads = jnp.stack([key_terms, value_terms]).reshape(
        2, head_count, block_count, slot_total, block_rows, head_width
    )
    no_pad = (0, 0)
    frame_sum = jnp.pad(grads[:, :, :, 0], (no_pad, no_pad, (0, 2), no_pad, no_pad))
    frame_sum = frame_sum + jnp.pad(grads[:, :, :, 1], (no_pad, no_pad, (1, 1), no_pad, no_pad))
    frame_sum = frame_sum + jnp.pad(grads[:, :, :, 2], (no_pad, no_pad, (2, 0), no_pad, no_pad))
    own_grads = frame_sum[:, :, 1 : block_count + 1]
    rim_parts = jnp.concatenate([frame_sum[:, :, 0], frame_sum[:, :, block_count + 1]], axis=2)
    rim_back = with_halo(rim_parts.astype(jnp.bfloat16), (("seq", 2),), block_rows).astype(
        rim_parts.dtype
    )
    own_grads = own_grads.at[:, :, 0].add(rim_back[:, :, 0:block_rows])
    own_grads = own_grads.at[:, :, block_count - 1].add(
        rim_back[:, :, 3 * block_rows : 4 * block_rows]
    )
    global_part = jnp.sum(grads[:, :, :, 3 : 3 + global_count], axis=2)
    global_total = lax.psum(global_part, "seq")
    global_onehot = (
        (global_local[:, None] == block_range[None, :]) & (global_owner == device)[:, None]
    ).astype(jnp.float32)
    own_grads = own_grads + jnp.einsum(
        "gn,chgbd->chnbd", global_onehot, global_total, precision=lax.Precision.HIGHEST
    )
    random_part = grads[:, :, :, 3 + global_count :]
    local_float = (random_local[..., None] == block_range).astype(jnp.float32)
    send_back = jnp.einsum(
        "hqjl,chqjbd->jchlbd", local_float, random_part, precision=lax.Precision.HIGHEST
    )
    send_back = send_back.astype(jnp.bfloat16).reshape(
        slot_count, 2, head_count, row_count, head_width
    )
    pieces = []
    for slot_index in range(slot_count):
        moving = send_back[slot_index]
        for bit_index in sections:
            arrived = swapped(moving, "seq", bit_index)
            flag_now = jnp.right_shift(xor_masks[:, slot_index], bit_index) & 1 == 1
            moving = jnp.where(flag_now[None, :, None, None], arrived, moving)
        pieces.append(moving)
    returned = jnp.stack(pieces)
    returned_sum = jnp.sum(returned.astype(jnp.float32), axis=0).reshape(
        2, head_count, block_count, block_rows, head_width
    )
    own_grads = own_grads + returned_sum
    grad_queries = grad_query.reshape(head_count, row_count, head_width).astype(jnp.bfloat16)
    grad_keys = own_grads[0].reshape(head_count, row_count, head_width).astype(jnp.bfloat16)
    grad_values = own_grads[1].reshape(head_count, row_count, head_width).astype(jnp.bfloat16)
    return (grad_queries, grad_keys, grad_values)


def on_device(queries, keys, values, grad_out, rand_ids, global_ids):
    count = lax.axis_size("seq")
    rows, width = queries.shape[1:]
    gathered_bytes = 4 * count * queries.size * queries.dtype.itemsize
    if gathered_bytes <= GATHER_BYTES and count & (count - 1) == 0 and count > GROUP and rows == width:
        return gathered(queries, keys, values, grad_out, rand_ids, global_ids)
    return routed(queries, keys, values, grad_out, rand_ids, global_ids)


def solution(mesh):
    in_specs = (
        P("head", "seq", None),
        P("head", "seq", None),
        P("head", "seq", None),
        P("head", "seq", None),
        P("head", "seq", None),
        P(),
    )
    out_specs = (P("head", "seq", None), P("head", "seq", None), P("head", "seq", None))
    return jax.shard_map(
        on_device, mesh=mesh, in_specs=in_specs, out_specs=out_specs, check_vma=False
    )
```

```python
import functools
import math

import jax
import jax.numpy as jnp
from jax import lax
from jax.experimental import pallas as pl
from jax.experimental.pallas import tpu as pltpu
from jax.sharding import PartitionSpec as P


GATHER_BYTES = 8 * 2**20
KERNEL_VMEM = 16 * 2**20
LOG2E = math.log2(math.e)
NEVER = -1e30
GROUP = 4
NT = (((1,), (1,)), ((), ()))


def pack_kernel(sizes, ids_hbm, gids_hbm, k_ref, v_ref, q_ref, g_ref, a_ref, b_ref, ids_ref, gids_ref, sems):
    heads, _, rows, _, block_rows, slots, _ = sizes
    blocks = rows // block_rows
    small = [
        pltpu.make_async_copy(ids_hbm, ids_ref, sems.at[0]),
        pltpu.make_async_copy(gids_hbm, gids_ref, sems.at[1]),
    ]
    copies = []
    for i, (src, dst, first) in enumerate(
        ((k_ref, a_ref, 0), (v_ref, a_ref, heads), (q_ref, b_ref, 0), (g_ref, b_ref, heads))
    ):
        for h in range(heads):
            place = pl.ds((first + h) * rows, rows)
            copies.append(pltpu.make_async_copy(src.at[h], dst.at[place], sems.at[2 + i * heads + h]))
    for c in small + copies:
        c.start()
    shape = (b_ref.shape[0] - 2 * heads * rows, rows)
    row = lax.broadcasted_iota(jnp.int32, shape, 0)
    lane = lax.broadcasted_iota(jnp.int32, shape, 1)
    block = jnp.zeros_like(lane)
    for n in range(1, blocks):
        block = block + jnp.where(lane >= n * block_rows, 1, 0)
    tile = lax.axis_index("seq") * blocks + block
    for c in small:
        c.wait()
    for h in range(heads):
        for j in range(slots):
            ids = jnp.full_like(lane, ids_ref[h, 0, j])
            for n in range(1, blocks):
                ids = jnp.where(block == n, ids_ref[h, n, j], ids)
            tile = jnp.where(row == h * slots + j, ids, tile)
    for n in range(gids_ref.shape[0]):
        tile = jnp.where(row == heads * slots + 1 + n, gids_ref[n], tile)
    b_ref[2 * heads * rows :] = tile.astype(jnp.float32).astype(jnp.bfloat16)
    for c in copies:
        c.wait()


class Shards:
    def __init__(self, sizes, a_refs, b_refs):
        self.heads, self.count, self.rows, self.width, self.block_rows, self.slots, self.gids = sizes
        self.blocks = self.rows // self.block_rows
        self.a, self.b = a_refs, b_refs
        self.scale = 1.0 / math.sqrt(self.width)
        self.rate = self.scale * LOG2E
        self.query_heads = [self.head(x) for x in b_refs]

    def part(self, refs, index, group):
        found = [refs[s][index * self.rows : (index + 1) * self.rows] for s in group]
        return found[0] if len(found) == 1 else jnp.concatenate(found)

    def k(self, h, group):
        return self.part(self.a, h, group)

    def v(self, h, group):
        return self.part(self.a, self.heads + h, group)

    def q(self, h, group):
        return self.part(self.b, h, group)

    def g(self, h, group):
        return self.part(self.b, self.heads + h, group)

    def key_ids(self, distances):
        shape = (len(distances) * self.blocks, self.rows)
        row = lax.broadcasted_iota(jnp.int32, shape, 0)
        me = lax.axis_index("seq")
        nk = jnp.zeros(shape, jnp.int32)
        for i, m in enumerate(distances):
            nk = jnp.where(row >= i * self.blocks, row + ((me ^ m) - i) * self.blocks, nk)
        nk = nk.astype(jnp.float32)
        seen = jnp.zeros(shape, jnp.float32)
        first = self.heads * self.slots + 1
        for n in range(self.gids):
            seen = seen + jnp.where(nk == self.query_heads[0][first + n : first + n + 1], 1.0, 0.0)
        return nk, seen

    def head(self, ref):
        return ref[2 * self.heads * self.rows :].astype(jnp.float32)

    def bias(self, keys, group):
        nk, seen = keys
        out = []
        for h in range(self.heads):
            cols = []
            for s in group:
                head = self.query_heads[s]
                nq = head[self.heads * self.slots : self.heads * self.slots + 1]
                count = seen + jnp.where(jnp.abs(nk - nq) <= 1.0, 1.0, 0.0)
                for j in range(self.slots):
                    r = h * self.slots + j
                    count = count + jnp.where(nk == head[r : r + 1], 1.0, 0.0)
                cols.append(jnp.where(count > 0.5, jnp.log2(jnp.maximum(count, 1.0)), NEVER))
            out.append(cols[0] if len(cols) == 1 else jnp.concatenate(cols, axis=1))
        return out

    def scores(self, h, keys, queries):
        return (
            lax.dot_general(self.k(h, keys), self.q(h, queries), NT, preferred_element_type=jnp.float32),
            lax.dot_general(self.v(h, keys), self.g(h, queries), NT, preferred_element_type=jnp.float32),
        )

    def stats(self, scored, bias, keep, start=None):
        s, dp = scored
        lanes = s.shape[1]
        steps = self.block_rows // 8
        top = None
        for kb in range(bias.shape[0]):
            x = s[kb * self.block_rows : (kb + 1) * self.block_rows] * self.rate + bias[kb : kb + 1]
            x = jnp.max(x.reshape(steps, 8, lanes), axis=0)
            top = x if top is None else jnp.maximum(top, x)
        top = jnp.maximum(jnp.max(top, axis=0, keepdims=True), 0.5 * NEVER)
        if start:
            top = jnp.maximum(top, start[0])
        acc_l = acc_d = None
        for kb in range(bias.shape[0]):
            cut = slice(kb * self.block_rows, (kb + 1) * self.block_rows)
            e = jnp.exp2(s[cut] * self.rate + (bias[kb : kb + 1] - top))
            keep(kb, cut, e, dp[cut])
            d = jnp.sum((e * dp[cut]).reshape(steps, 8, lanes), axis=0)
            e = jnp.sum(e.reshape(steps, 8, lanes), axis=0)
            acc_l = e if acc_l is None else acc_l + e
            acc_d = d if acc_d is None else acc_d + d
        acc_l, acc_d = (jnp.sum(x, axis=0, keepdims=True) for x in (acc_l, acc_d))
        if start:
            w = jnp.exp2(start[0] - top)
            acc_l, acc_d = acc_l + start[1] * w, acc_d + start[2] * w
        return top, acc_l, acc_d


def stats_kernel(sizes, distances, n_queries, *refs):
    n_keys = len(distances)
    a_refs, b_refs = refs[:n_keys], refs[n_keys : n_keys + n_queries]
    before = refs[n_keys + n_queries : -3]
    stat, e_ref, dp_ref = refs[-3:]
    sh = Shards(sizes, a_refs, b_refs)
    keys, queries = list(range(n_keys)), list(range(n_queries))
    bias = sh.bias(sh.key_ids(distances), queries)
    scored = [sh.scores(h, keys, queries) for h in range(sh.heads)]
    for h in range(sh.heads):

        def keep(kb, cut, e, dp):
            e_ref[h, cut] = e
            dp_ref[h, cut] = dp

        start = [before[0][3 * h + i : 3 * h + i + 1] for i in range(3)] if before else None
        for i, x in enumerate(sh.stats(scored[h], bias[h], keep, start)):
            stat[3 * h + i : 3 * h + i + 1] = x


def kept_tiles(sh, kept, stat, h, lanes, shift=None):
    first, e_first, dp_first, e_last, dp_last = kept
    row = slice(3 * h, 3 * h + 1)
    top = stat[row, lanes]
    base = top if shift is None else shift
    for before, e_ref, dp_ref in ((first[row, lanes], e_first, dp_first), (top, e_last, dp_last)):
        w = None if before is base else jnp.exp2(before - base)
        for r in range(0, e_ref.shape[1], sh.block_rows):
            cut = slice(r, r + sh.block_rows)
            e = e_ref[h, cut, lanes]
            yield (e if w is None else e * w), dp_ref[h, cut, lanes]


def partner_kernel(sizes, widths, *refs):
    heads, rows = sizes[0], sizes[2]
    n_keys, n_queries = widths
    a_refs, stat, kept = refs[:n_keys], refs[n_keys], refs[n_keys + 1 : n_keys + 6]
    outs = refs[n_keys + 6 :]
    sh = Shards(sizes, a_refs, ())
    tn = (((0,), (0,)), ((), ()))
    for s in range(1, n_queries):
        lanes = slice(s * rows, (s + 1) * rows)
        for h in range(heads):
            k = sh.k(h, list(range(n_keys)))
            local = local_dot(stat, h, lanes)
            low, e_low = [], []
            for e, dp in kept_tiles(sh, kept, stat, h, lanes):
                e_low.append(e.astype(jnp.bfloat16))
                low.append((e * (dp - local)).astype(jnp.bfloat16))
            for i, x in enumerate((low, e_low)):
                x = lax.dot_general(jnp.concatenate(x), k, tn, preferred_element_type=jnp.float32)
                outs[s - 1][(i * heads + h) * rows : (i * heads + h + 1) * rows] = x.astype(outs[s - 1].dtype)


def local_dot(stat, h, lanes):
    total = stat[3 * h + 1 : 3 * h + 2, lanes]
    return stat[3 * h + 2 : 3 * h + 3, lanes] / jnp.where(total > 0.0, total, 1.0)


def whole_stats(stats, rows, h, s):
    holders = range(len(stats))

    def part(i, p):
        return stats[p][3 * h + i : 3 * h + i + 1, (s ^ p) * rows : ((s ^ p) + 1) * rows]

    top = functools.reduce(jnp.maximum, [part(0, p) for p in holders])
    scales = [jnp.exp2(part(0, p) - top) for p in holders]
    total = sum(part(1, p) * w for p, w in zip(holders, scales))
    weighted = sum(part(2, p) * w for p, w in zip(holders, scales))
    return top + jnp.log2(total), weighted / total


def grads_kernel(sizes, widths, *refs):
    heads, rows = sizes[0], sizes[2]
    n_keys, n_queries = widths
    b_refs = refs[:n_queries]
    stats, kept = refs[n_queries : 2 * n_queries], refs[2 * n_queries : 2 * n_queries + 5]
    kv_out = refs[2 * n_queries + 5 :]
    sh = Shards(sizes, (), b_refs)
    queries = list(range(n_queries))
    for h in range(heads):
        whole = [whole_stats(stats, rows, h, s) for s in queries]
        shift, dots = (jnp.concatenate([x[i] for x in whole], axis=1) for i in range(2))
        p_low, ds_low = [], []
        for p, dp in kept_tiles(sh, kept, stats[0], h, slice(0, n_queries * rows), shift):
            p_low.append(p.astype(jnp.bfloat16))
            ds_low.append((p * (dp - dots)).astype(jnp.bfloat16))
        dk = jnp.dot(jnp.concatenate(ds_low), sh.q(h, queries), preferred_element_type=jnp.float32) * sh.scale
        dv = jnp.dot(jnp.concatenate(p_low), sh.g(h, queries), preferred_element_type=jnp.float32)
        for m in range(n_keys):
            cut = slice(m * rows, (m + 1) * rows)
            kv_out[m][h * rows : (h + 1) * rows] = dk[cut].astype(kv_out[m].dtype)
            kv_out[m][(heads + h) * rows : (heads + h + 1) * rows] = dv[cut].astype(kv_out[m].dtype)


def queries_kernel(sizes, widths, *refs):
    heads, rows = sizes[0], sizes[2]
    n_keys, n_queries = widths
    a_refs, refs = refs[:n_keys], refs[n_keys:]
    stats, kept, refs = refs[:n_queries], refs[n_queries : n_queries + 5], refs[n_queries + 5 :]
    sums, out = refs[: n_queries - 1], refs[-1]
    sh = Shards(sizes, a_refs, ())
    for h in range(heads):
        shift, dots = whole_stats(stats, rows, h, 0)
        low = []
        for p, dp in kept_tiles(sh, kept, stats[0], h, slice(0, rows), shift):
            low.append((p * (dp - dots)).astype(jnp.bfloat16))
        dq = lax.dot_general(
            jnp.concatenate(low), sh.k(h, list(range(n_keys))), (((0,), (0,)), ((), ())),
            preferred_element_type=jnp.float32,
        )
        for p in range(1, n_queries):
            lanes = slice(p * rows, (p + 1) * rows)
            w = jnp.exp2(stats[p][3 * h : 3 * h + 1, lanes] - shift)
            moved = w * (local_dot(stats[p], h, lanes) - dots)
            w, moved = (jnp.broadcast_to(x, (rows, rows)).T for x in (w, moved))
            first = sums[p - 1][h * rows : (h + 1) * rows].astype(jnp.float32)
            second = sums[p - 1][(heads + h) * rows : (heads + h + 1) * rows].astype(jnp.float32)
            dq = dq + (first * w + second * moved)
        out[h] = (dq * sh.scale).astype(out.dtype)


def sum_kernel(sizes, n_keys, *refs):
    heads, rows = sizes[0], sizes[2]
    parts, outs, bufs, sems = refs[:n_keys], refs[n_keys : n_keys + 2], refs[n_keys + 2 : -1], refs[-1]
    copies = []
    for i in range(2):
        for h in range(heads):
            cut = slice((i * heads + h) * rows, (i * heads + h + 1) * rows)
            total = sum(p[cut].astype(jnp.float32) for p in parts)
            bufs[i][h] = total.astype(bufs[i].dtype)
        copies.append(pltpu.make_async_copy(bufs[i], outs[i], sems.at[i]))
        copies[-1].start()
    for c in copies:
        c.wait()


def near(arrays):
    return [pltpu.with_memory_space_constraint(x, pltpu.VMEM) for x in arrays]


def exchanged(value, mask):
    return lax.ppermute(value, "seq", [(i, i ^ mask) for i in range(lax.axis_size("seq"))])


def key_moves(n_keys):
    direct = [m for m in range(n_keys - 1, 0, -1) if m & (m - 1) == 0]
    relayed = [m for m in range(1, n_keys) if m not in direct]
    return [(m, m) for m in direct], [(m, m & -m) for m in relayed]


def gathered(queries, keys, values, grad_out, rand_ids, global_ids):
    heads, rows, width = queries.shape
    blocks, slots = rand_ids.shape[1:]
    count = lax.axis_size("seq")
    n_keys = min(GROUP, count)
    n_queries = count // n_keys
    widths = (n_keys, n_queries)
    sizes = (heads, count, rows, width, rows // blocks, slots, global_ids.shape[0])
    head_rows = -(-(heads * slots + 1 + global_ids.shape[0]) // 16) * 16
    vmem = pl.BlockSpec(memory_space=pltpu.VMEM)
    anyspace = pl.BlockSpec(memory_space=pl.ANY)
    params = pltpu.CompilerParams(vmem_limit_bytes=KERNEL_VMEM)
    head_rows = -(-(heads * slots + 1 + global_ids.shape[0]) // 16) * 16
    a, b = pl.pallas_call(
        functools.partial(pack_kernel, sizes),
        out_shape=(
            pltpu.VMEM((2 * heads * rows, width), queries.dtype),
            pltpu.VMEM((2 * heads * rows + head_rows, width), queries.dtype),
        ),
        in_specs=[anyspace] * 6,
        out_specs=(vmem, vmem),
        scratch_shapes=[
            pltpu.SMEM(rand_ids.shape, jnp.int32),
            pltpu.SMEM(global_ids.shape, jnp.int32),
            pltpu.SemaphoreType.DMA((2 + 4 * heads,)),
        ],
    )(rand_ids, global_ids, keys, values, queries, grad_out)

    b_all = [b] + [exchanged(b, s * n_keys) for s in range(1, n_queries)]
    a_all = {0: a}
    for moves in key_moves(n_keys):
        for m, last in moves:
            a_all[m] = exchanged(a_all[m - last], last)
    a_all = [a_all[m] for m in range(n_keys)]
    lanes = n_queries * rows
    stat_rows = -(-3 * heads // 8) * 8
    order = [0] + [m for moves in key_moves(n_keys) for m in sorted(m for m, _ in moves)]
    a_all = near([a_all[m] for m in order])
    b_all = near(b_all)
    n_first = 1 + len(key_moves(n_keys)[0])
    stat, kept = None, []
    for here in (slice(0, n_first), slice(n_first, n_keys)):
        part = a_all[here]
        before = near([stat]) if kept else []
        stat, e, dp = pl.pallas_call(
            functools.partial(stats_kernel, sizes, order[here], n_queries),
            out_shape=(pltpu.VMEM((stat_rows, lanes), jnp.float32),)
            + (pltpu.VMEM((heads, len(part) * rows, lanes), jnp.float32),) * 2,
            compiler_params=params,
            in_specs=[vmem] * (len(part) + n_queries + len(before)),
            out_specs=(vmem,) * 3,
        )(*part, *b_all, *before)
        kept += ([] if kept else [stat]) + [e, dp]
    kept = near(kept)
    stats = [stat] + [exchanged(stat, s * n_keys) for s in range(1, n_queries)]
    sums = pl.pallas_call(
        functools.partial(partner_kernel, sizes, widths),
        out_shape=(pltpu.VMEM((2 * heads * rows, width), queries.dtype),) * (n_queries - 1),
        compiler_params=params,
        in_specs=[vmem] * (n_keys + 6),
        out_specs=(vmem,) * (n_queries - 1),
    )(*a_all, *near([stat]), *kept)
    sums = [exchanged(x, s * n_keys) for s, x in zip(range(1, n_queries), sums)]
    shapes = [pltpu.VMEM((2 * heads * rows, width), jnp.float32)]
    shapes += [pltpu.VMEM((2 * heads * rows, width), queries.dtype)] * (n_keys - 1)
    parts = pl.pallas_call(
        functools.partial(grads_kernel, sizes, widths),
        out_shape=tuple(shapes),
        compiler_params=params,
        in_specs=[vmem] * (2 * n_queries + 5),
        out_specs=(vmem,) * len(shapes),
    )(*b_all, *near(stats), *kept)
    parts = [parts[0]] + [exchanged(x, m) for m, x in zip(order[1:], parts[1:])]
    out = jax.ShapeDtypeStruct(queries.shape, queries.dtype)
    grad_queries = pl.pallas_call(
        functools.partial(queries_kernel, sizes, widths),
        out_shape=out,
        compiler_params=params,
        in_specs=[vmem] * (n_keys + 2 * n_queries + 4),
        out_specs=vmem,
    )(*a_all, *near(stats), *kept, *near(sums))
    buf = pltpu.VMEM(queries.shape, queries.dtype)
    grad_keys, grad_values = pl.pallas_call(
        functools.partial(sum_kernel, sizes, n_keys),
        out_shape=(out, out),
        compiler_params=params,
        in_specs=[vmem] * n_keys,
        out_specs=(anyspace,) * 2,
        scratch_shapes=[buf, buf, pltpu.SemaphoreType.DMA((2,))],
    )(*near(parts))
    return grad_queries, grad_keys, grad_values


def with_halo(value, sides, width):
    for axis, dim in sides:
        peers, length = (lax.axis_size(axis), value.shape[dim])
        up = [(i, (i + 1) % peers) for i in range(peers - 1)]
        down = [(j, i) for i, j in up]
        last = lax.slice_in_dim(value, length - width, length, axis=dim)
        initial = lax.slice_in_dim(value, 0, width, axis=dim)
        before = lax.ppermute(last, axis, up)
        after = lax.ppermute(initial, axis, down)
        value = jnp.concatenate([before, value, after], axis=dim)
    return value


def swapped(value, axis, distance):
    mask = 2**distance
    pairs = [(source, source ^ mask) for source in range(lax.axis_size(axis))]
    return lax.ppermute(value, axis, pairs)


def section_list(section_count):
    return list(range(section_count))


def routed(queries, keys, values, grad_out, rand_ids, global_ids):
    head_count, row_count, head_width = queries.shape
    block_count = rand_ids.shape[1]
    slot_count = rand_ids.shape[2]
    block_rows = row_count // block_count
    global_count = global_ids.shape[0]
    slot_total = 3 + global_count + slot_count
    device = lax.axis_index("seq")
    seq_count = lax.axis_size("seq")
    sections = section_list(seq_count.bit_length() - 1)
    score_scale = 1.0 / math.sqrt(head_width)
    key_vals = jnp.stack([keys, values])
    padded = with_halo(key_vals, (("seq", 2),), block_rows)
    padded_blocks = padded.reshape(2, head_count, block_count + 2, block_rows, head_width)
    window = jnp.stack(
        [
            padded_blocks[:, :, 0:block_count],
            padded_blocks[:, :, 1 : block_count + 1],
            padded_blocks[:, :, 2 : block_count + 2],
        ],
        3,
    )
    key_blocks = key_vals.reshape(2, head_count, block_count, block_rows, head_width)
    global_local = global_ids % block_count
    global_owner = global_ids // block_count
    owned = (global_owner == device).astype(jnp.float32)
    picked = jnp.take(key_blocks, global_local, axis=2).astype(jnp.float32)
    global_sum = lax.psum(picked * owned[None, None, :, None, None], "seq")
    global_kv = global_sum.astype(jnp.bfloat16)
    global_keys = jnp.broadcast_to(
        global_kv[:, :, None], (2, head_count, block_count, global_count, block_rows, head_width)
    )
    xor_masks = jnp.bitwise_xor(rand_ids[:, 0, :] // block_count, device)
    pieces = []
    for slot_index in range(slot_count):
        moving = key_vals
        for bit_index in sections:
            arrived = swapped(moving, "seq", bit_index)
            flag_now = jnp.right_shift(xor_masks[:, slot_index], bit_index) & 1 == 1
            moving = jnp.where(flag_now[None, :, None, None], arrived, moving)
        pieces.append(moving)
    routed = jnp.stack(pieces)
    routed_blocks = routed.reshape(slot_count, 2, head_count, block_count, block_rows, head_width)
    random_local = rand_ids % block_count
    local_onehot = (random_local[..., None] == jnp.arange(block_count, dtype=jnp.int32)).astype(
        jnp.bfloat16
    )
    random_keys = jnp.einsum(
        "hqjl,jchlbd->chqjbd", local_onehot, routed_blocks, preferred_element_type=jnp.float32
    ).astype(jnp.bfloat16)
    all_keys = jnp.concatenate([window, global_keys, random_keys], axis=3)
    key_list = all_keys[0].reshape(head_count, block_count, slot_total * block_rows, head_width)
    value_list = all_keys[1].reshape(head_count, block_count, slot_total * block_rows, head_width)
    block_range = jnp.arange(block_count, dtype=jnp.int32)
    left_valid = jnp.logical_not((block_range == 0) & (device == 0))
    right_valid = jnp.logical_not((block_range == block_count - 1) & (device == seq_count - 1))
    valid = jnp.concatenate(
        [
            left_valid[:, None],
            jnp.ones((block_count, 1), bool),
            right_valid[:, None],
            jnp.ones((block_count, global_count + slot_count), bool),
        ],
        1,
    )
    mask = jnp.repeat(valid, block_rows, axis=1)[None, :, None, :]
    query_blocks = queries.reshape(head_count, block_count, block_rows, head_width)
    grad_blocks = grad_out.reshape(head_count, block_count, block_rows, head_width)
    scores = (
        jnp.einsum("hnqd,hnkd->hnqk", query_blocks, key_list, preferred_element_type=jnp.float32)
        * score_scale
    )
    row_max = jnp.max(jnp.where(mask, scores, -1e30), -1)
    total = jnp.sum(jnp.where(mask, jnp.exp(scores - row_max[..., None]), 0.0), -1)
    log_total = row_max + jnp.log(total)
    probs = jnp.where(mask, jnp.exp(scores - log_total[..., None]), 0.0)
    probs_low = probs.astype(jnp.bfloat16)
    output = jnp.einsum(
        "hnqk,hnkd->hnqd", probs_low, value_list, preferred_element_type=jnp.float32
    )
    row_dot = jnp.sum(grad_blocks.astype(jnp.float32) * output, -1)
    grad_probs = jnp.einsum(
        "hnqd,hnkd->hnqk", grad_blocks, value_list, preferred_element_type=jnp.float32
    )
    scores_low = (probs * (grad_probs - row_dot[..., None])).astype(jnp.bfloat16)
    grad_query = score_scale * jnp.einsum(
        "hnqk,hnkd->hnqd", scores_low, key_list, preferred_element_type=jnp.float32
    )
    key_terms = score_scale * jnp.einsum(
        "hnqk,hnqd->hnkd", scores_low, query_blocks, preferred_element_type=jnp.float32
    )
    value_terms = jnp.einsum(
        "hnqk,hnqd->hnkd", probs_low, grad_blocks, preferred_element_type=jnp.float32
    )
    grads = jnp.stack([key_terms, value_terms]).reshape(
        2, head_count, block_count, slot_total, block_rows, head_width
    )
    no_pad = (0, 0)
    frame_sum = jnp.pad(grads[:, :, :, 0], (no_pad, no_pad, (0, 2), no_pad, no_pad))
    frame_sum = frame_sum + jnp.pad(grads[:, :, :, 1], (no_pad, no_pad, (1, 1), no_pad, no_pad))
    frame_sum = frame_sum + jnp.pad(grads[:, :, :, 2], (no_pad, no_pad, (2, 0), no_pad, no_pad))
    own_grads = frame_sum[:, :, 1 : block_count + 1]
    rim_parts = jnp.concatenate([frame_sum[:, :, 0], frame_sum[:, :, block_count + 1]], axis=2)
    rim_back = with_halo(rim_parts.astype(jnp.bfloat16), (("seq", 2),), block_rows).astype(
        rim_parts.dtype
    )
    own_grads = own_grads.at[:, :, 0].add(rim_back[:, :, 0:block_rows])
    own_grads = own_grads.at[:, :, block_count - 1].add(
        rim_back[:, :, 3 * block_rows : 4 * block_rows]
    )
    global_part = jnp.sum(grads[:, :, :, 3 : 3 + global_count], axis=2)
    global_total = lax.psum(global_part, "seq")
    global_onehot = (
        (global_local[:, None] == block_range[None, :]) & (global_owner == device)[:, None]
    ).astype(jnp.float32)
    own_grads = own_grads + jnp.einsum(
        "gn,chgbd->chnbd", global_onehot, global_total, precision=lax.Precision.HIGHEST
    )
    random_part = grads[:, :, :, 3 + global_count :]
    local_float = (random_local[..., None] == block_range).astype(jnp.float32)
    send_back = jnp.einsum(
        "hqjl,chqjbd->jchlbd", local_float, random_part, precision=lax.Precision.HIGHEST
    )
    send_back = send_back.astype(jnp.bfloat16).reshape(
        slot_count, 2, head_count, row_count, head_width
    )
    pieces = []
    for slot_index in range(slot_count):
        moving = send_back[slot_index]
        for bit_index in sections:
            arrived = swapped(moving, "seq", bit_index)
            flag_now = jnp.right_shift(xor_masks[:, slot_index], bit_index) & 1 == 1
            moving = jnp.where(flag_now[None, :, None, None], arrived, moving)
        pieces.append(moving)
    returned = jnp.stack(pieces)
    returned_sum = jnp.sum(returned.astype(jnp.float32), axis=0).reshape(
        2, head_count, block_count, block_rows, head_width
    )
    own_grads = own_grads + returned_sum
    grad_queries = grad_query.reshape(head_count, row_count, head_width).astype(jnp.bfloat16)
    grad_keys = own_grads[0].reshape(head_count, row_count, head_width).astype(jnp.bfloat16)
    grad_values = own_grads[1].reshape(head_count, row_count, head_width).astype(jnp.bfloat16)
    return (grad_queries, grad_keys, grad_values)


def on_device(queries, keys, values, grad_out, rand_ids, global_ids):
    count = lax.axis_size("seq")
    rows, width = queries.shape[1:]
    gathered_bytes = 4 * count * queries.size * queries.dtype.itemsize
    if gathered_bytes <= GATHER_BYTES and count & (count - 1) == 0 and count > GROUP and rows == width:
        return gathered(queries, keys, values, grad_out, rand_ids, global_ids)
    return routed(queries, keys, values, grad_out, rand_ids, global_ids)


def solution(mesh):
    in_specs = (
        P("head", "seq", None),
        P("head", "seq", None),
        P("head", "seq", None),
        P("head", "seq", None),
        P("head", "seq", None),
        P(),
    )
    out_specs = (P("head", "seq", None), P("head", "seq", None), P("head", "seq", None))
    return jax.shard_map(
        on_device, mesh=mesh, in_specs=in_specs, out_specs=out_specs, check_vma=False
    )
```

```python
import functools
import math

import jax
import jax.numpy as jnp
from jax import lax
from jax.experimental import pallas as pl
from jax.experimental.pallas import tpu as pltpu
from jax.sharding import PartitionSpec as P


GATHER_BYTES = 8 * 2**20
KERNEL_VMEM = 16 * 2**20
LOG2E = math.log2(math.e)
NEVER = -1e30
GROUP = 4
NT = (((1,), (1,)), ((), ()))


def pack_kernel(sizes, ids_hbm, gids_hbm, k_ref, v_ref, q_ref, g_ref, a_ref, b_ref, ids_ref, gids_ref, sems):
    heads, _, rows, _, block_rows, slots, _ = sizes
    blocks = rows // block_rows
    small = [
        pltpu.make_async_copy(ids_hbm, ids_ref, sems.at[0]),
        pltpu.make_async_copy(gids_hbm, gids_ref, sems.at[1]),
    ]
    copies = []
    for i, (src, dst, first) in enumerate(
        ((k_ref, a_ref, 0), (v_ref, a_ref, heads), (q_ref, b_ref, 0), (g_ref, b_ref, heads))
    ):
        for h in range(heads):
            place = pl.ds((first + h) * rows, rows)
            copies.append(pltpu.make_async_copy(src.at[h], dst.at[place], sems.at[2 + i * heads + h]))
    for c in small + copies:
        c.start()
    shape = (b_ref.shape[0] - 2 * heads * rows, rows)
    row = lax.broadcasted_iota(jnp.int32, shape, 0)
    lane = lax.broadcasted_iota(jnp.int32, shape, 1)
    block = jnp.zeros_like(lane)
    for n in range(1, blocks):
        block = block + jnp.where(lane >= n * block_rows, 1, 0)
    tile = lax.axis_index("seq") * blocks + block
    for c in small:
        c.wait()
    for h in range(heads):
        for j in range(slots):
            ids = jnp.full_like(lane, ids_ref[h, 0, j])
            for n in range(1, blocks):
                ids = jnp.where(block == n, ids_ref[h, n, j], ids)
            tile = jnp.where(row == h * slots + j, ids, tile)
    for n in range(gids_ref.shape[0]):
        tile = jnp.where(row == heads * slots + 1 + n, gids_ref[n], tile)
    b_ref[2 * heads * rows :] = tile.astype(jnp.float32).astype(jnp.bfloat16)
    for c in copies:
        c.wait()


class Shards:
    def __init__(self, sizes, a_refs, b_refs):
        self.heads, self.count, self.rows, self.width, self.block_rows, self.slots, self.gids = sizes
        self.blocks = self.rows // self.block_rows
        self.a, self.b = a_refs, b_refs
        self.scale = 1.0 / math.sqrt(self.width)
        self.rate = self.scale * LOG2E
        self.query_heads = [self.head(x) for x in b_refs]

    def part(self, refs, index, group):
        found = [refs[s][index * self.rows : (index + 1) * self.rows] for s in group]
        return found[0] if len(found) == 1 else jnp.concatenate(found)

    def k(self, h, group):
        return self.part(self.a, h, group)

    def v(self, h, group):
        return self.part(self.a, self.heads + h, group)

    def q(self, h, group):
        return self.part(self.b, h, group)

    def g(self, h, group):
        return self.part(self.b, self.heads + h, group)

    def key_ids(self, distances):
        shape = (len(distances) * self.blocks, self.rows)
        row = lax.broadcasted_iota(jnp.int32, shape, 0)
        me = lax.axis_index("seq")
        nk = jnp.zeros(shape, jnp.int32)
        for i, m in enumerate(distances):
            nk = jnp.where(row >= i * self.blocks, row + ((me ^ m) - i) * self.blocks, nk)
        nk = nk.astype(jnp.float32)
        seen = jnp.zeros(shape, jnp.float32)
        first = self.heads * self.slots + 1
        for n in range(self.gids):
            seen = seen + jnp.where(nk == self.query_heads[0][first + n : first + n + 1], 1.0, 0.0)
        return nk, seen

    def head(self, ref):
        return ref[2 * self.heads * self.rows :].astype(jnp.float32)

    def bias(self, keys, group):
        nk, seen = keys
        out = []
        for h in range(self.heads):
            cols = []
            for s in group:
                head = self.query_heads[s]
                nq = head[self.heads * self.slots : self.heads * self.slots + 1]
                count = seen + jnp.where(jnp.abs(nk - nq) <= 1.0, 1.0, 0.0)
                for j in range(self.slots):
                    r = h * self.slots + j
                    count = count + jnp.where(nk == head[r : r + 1], 1.0, 0.0)
                cols.append(jnp.where(count > 0.5, jnp.log2(jnp.maximum(count, 1.0)), NEVER))
            out.append(cols[0] if len(cols) == 1 else jnp.concatenate(cols, axis=1))
        return out

    def scores(self, h, keys, queries):
        return (
            lax.dot_general(self.k(h, keys), self.q(h, queries), NT, preferred_element_type=jnp.float32),
            lax.dot_general(self.v(h, keys), self.g(h, queries), NT, preferred_element_type=jnp.float32),
        )

    def stats(self, scored, bias, keep, start=None):
        s, dp = scored
        lanes = s.shape[1]
        steps = self.block_rows // 8
        top = None
        for kb in range(bias.shape[0]):
            x = s[kb * self.block_rows : (kb + 1) * self.block_rows] * self.rate + bias[kb : kb + 1]
            x = jnp.max(x.reshape(steps, 8, lanes), axis=0)
            top = x if top is None else jnp.maximum(top, x)
        top = jnp.maximum(jnp.max(top, axis=0, keepdims=True), 0.5 * NEVER)
        if start:
            top = jnp.maximum(top, start[0])
        acc_l = acc_d = None
        for kb in range(bias.shape[0]):
            cut = slice(kb * self.block_rows, (kb + 1) * self.block_rows)
            e = jnp.exp2(s[cut] * self.rate + (bias[kb : kb + 1] - top))
            keep(kb, cut, e, dp[cut])
            d = jnp.sum((e * dp[cut]).reshape(steps, 8, lanes), axis=0)
            e = jnp.sum(e.reshape(steps, 8, lanes), axis=0)
            acc_l = e if acc_l is None else acc_l + e
            acc_d = d if acc_d is None else acc_d + d
        acc_l, acc_d = (jnp.sum(x, axis=0, keepdims=True) for x in (acc_l, acc_d))
        if start:
            w = jnp.exp2(start[0] - top)
            acc_l, acc_d = acc_l + start[1] * w, acc_d + start[2] * w
        return top, acc_l, acc_d


def stats_kernel(sizes, distances, n_queries, *refs):
    n_keys = len(distances)
    a_refs, b_refs = refs[:n_keys], refs[n_keys : n_keys + n_queries]
    before = refs[n_keys + n_queries : -3]
    stat, e_ref, dp_ref = refs[-3:]
    sh = Shards(sizes, a_refs, b_refs)
    keys, queries = list(range(n_keys)), list(range(n_queries))
    bias = sh.bias(sh.key_ids(distances), queries)
    scored = [sh.scores(h, keys, queries) for h in range(sh.heads)]
    for h in range(sh.heads):

        def keep(kb, cut, e, dp):
            e_ref[h, cut] = e
            dp_ref[h, cut] = dp

        start = [before[0][3 * h + i : 3 * h + i + 1] for i in range(3)] if before else None
        for i, x in enumerate(sh.stats(scored[h], bias[h], keep, start)):
            stat[3 * h + i : 3 * h + i + 1] = x


def kept_tiles(sh, kept, stat, h, lanes, shift=None):
    first, e_first, dp_first, e_last, dp_last = kept
    row = slice(3 * h, 3 * h + 1)
    top = stat[row, lanes]
    base = top if shift is None else shift
    for before, e_ref, dp_ref in ((first[row, lanes], e_first, dp_first), (top, e_last, dp_last)):
        w = None if before is base else jnp.exp2(before - base)
        for r in range(0, e_ref.shape[1], sh.block_rows):
            cut = slice(r, r + sh.block_rows)
            e = e_ref[h, cut, lanes]
            yield (e if w is None else e * w), dp_ref[h, cut, lanes]


def partner_kernel(sizes, widths, *refs):
    heads, rows = sizes[0], sizes[2]
    n_keys, n_queries = widths
    a_refs, stat, kept = refs[:n_keys], refs[n_keys], refs[n_keys + 1 : n_keys + 6]
    outs = refs[n_keys + 6 :]
    sh = Shards(sizes, a_refs, ())
    tn = (((0,), (0,)), ((), ()))
    for s in range(1, n_queries):
        lanes = slice(s * rows, (s + 1) * rows)
        for h in range(heads):
            k = sh.k(h, list(range(n_keys)))
            local = local_dot(stat, h, lanes)
            low, e_low = [], []
            for e, dp in kept_tiles(sh, kept, stat, h, lanes):
                e_low.append(e.astype(jnp.bfloat16))
                low.append((e * (dp - local)).astype(jnp.bfloat16))
            for i, x in enumerate((low, e_low)):
                x = lax.dot_general(jnp.concatenate(x), k, tn, preferred_element_type=jnp.float32)
                outs[s - 1][(i * heads + h) * rows : (i * heads + h + 1) * rows] = x.astype(outs[s - 1].dtype)


def local_dot(stat, h, lanes):
    total = stat[3 * h + 1 : 3 * h + 2, lanes]
    return stat[3 * h + 2 : 3 * h + 3, lanes] / jnp.where(total > 0.0, total, 1.0)


def whole_stats(stats, rows, h, s):
    holders = range(len(stats))

    def part(i, p):
        return stats[p][3 * h + i : 3 * h + i + 1, (s ^ p) * rows : ((s ^ p) + 1) * rows]

    top = functools.reduce(jnp.maximum, [part(0, p) for p in holders])
    scales = [jnp.exp2(part(0, p) - top) for p in holders]
    total = sum(part(1, p) * w for p, w in zip(holders, scales))
    weighted = sum(part(2, p) * w for p, w in zip(holders, scales))
    return top + jnp.log2(total), weighted / total


def grads_kernel(sizes, widths, picked, *refs):
    heads, rows = sizes[0], sizes[2]
    _, n_queries = widths
    b_refs = refs[:n_queries]
    stats, kept = refs[n_queries : 2 * n_queries], refs[2 * n_queries : 2 * n_queries + 5]
    kv_out = refs[2 * n_queries + 5 :]
    sh = Shards(sizes, (), b_refs)
    queries = list(range(n_queries))
    for h in range(heads):
        whole = [whole_stats(stats, rows, h, s) for s in queries]
        shift, dots = (jnp.concatenate([x[i] for x in whole], axis=1) for i in range(2))
        p_low, ds_low = [], []
        tiles = list(kept_tiles(sh, kept, stats[0], h, slice(0, n_queries * rows), shift))
        for p, dp in tiles[picked.start * sh.blocks : picked.stop * sh.blocks]:
            p_low.append(p.astype(jnp.bfloat16))
            ds_low.append((p * (dp - dots)).astype(jnp.bfloat16))
        dk = jnp.dot(jnp.concatenate(ds_low), sh.q(h, queries), preferred_element_type=jnp.float32) * sh.scale
        dv = jnp.dot(jnp.concatenate(p_low), sh.g(h, queries), preferred_element_type=jnp.float32)
        for m in range(len(kv_out)):
            cut = slice(m * rows, (m + 1) * rows)
            kv_out[m][h * rows : (h + 1) * rows] = dk[cut].astype(kv_out[m].dtype)
            kv_out[m][(heads + h) * rows : (heads + h + 1) * rows] = dv[cut].astype(kv_out[m].dtype)


def queries_kernel(sizes, widths, *refs):
    heads, rows = sizes[0], sizes[2]
    n_keys, n_queries = widths
    a_refs, refs = refs[:n_keys], refs[n_keys:]
    stats, kept, refs = refs[:n_queries], refs[n_queries : n_queries + 5], refs[n_queries + 5 :]
    sums, out = refs[: n_queries - 1], refs[-1]
    sh = Shards(sizes, a_refs, ())
    for h in range(heads):
        shift, dots = whole_stats(stats, rows, h, 0)
        low = []
        for p, dp in kept_tiles(sh, kept, stats[0], h, slice(0, rows), shift):
            low.append((p * (dp - dots)).astype(jnp.bfloat16))
        dq = lax.dot_general(
            jnp.concatenate(low), sh.k(h, list(range(n_keys))), (((0,), (0,)), ((), ())),
            preferred_element_type=jnp.float32,
        )
        for p in range(1, n_queries):
            lanes = slice(p * rows, (p + 1) * rows)
            w = jnp.exp2(stats[p][3 * h : 3 * h + 1, lanes] - shift)
            moved = w * (local_dot(stats[p], h, lanes) - dots)
            w, moved = (jnp.broadcast_to(x, (rows, rows)).T for x in (w, moved))
            first = sums[p - 1][h * rows : (h + 1) * rows].astype(jnp.float32)
            second = sums[p - 1][(heads + h) * rows : (heads + h + 1) * rows].astype(jnp.float32)
            dq = dq + (first * w + second * moved)
        out[h] = (dq * sh.scale).astype(out.dtype)


def sum_kernel(sizes, n_keys, *refs):
    heads, rows = sizes[0], sizes[2]
    parts, outs, bufs, sems = refs[:n_keys], refs[n_keys : n_keys + 2], refs[n_keys + 2 : -1], refs[-1]
    copies = []
    for i in range(2):
        for h in range(heads):
            cut = slice((i * heads + h) * rows, (i * heads + h + 1) * rows)
            total = sum(p[cut].astype(jnp.float32) for p in parts)
            bufs[i][h] = total.astype(bufs[i].dtype)
            copies.append(pltpu.make_async_copy(bufs[i].at[h], outs[i].at[h], sems.at[i * heads + h]))
            copies[-1].start()
    for c in copies:
        c.wait()


def near(arrays):
    return [pltpu.with_memory_space_constraint(x, pltpu.VMEM) for x in arrays]


def exchanged(value, mask):
    return lax.ppermute(value, "seq", [(i, i ^ mask) for i in range(lax.axis_size("seq"))])


def key_moves(n_keys):
    direct = [m for m in range(n_keys - 1, 0, -1) if m & (m - 1) == 0]
    relayed = [m for m in range(1, n_keys) if m not in direct]
    return [(m, m) for m in direct], [(m, m & -m) for m in relayed]


def gathered(queries, keys, values, grad_out, rand_ids, global_ids):
    heads, rows, width = queries.shape
    blocks, slots = rand_ids.shape[1:]
    count = lax.axis_size("seq")
    n_keys = min(GROUP, count)
    n_queries = count // n_keys
    widths = (n_keys, n_queries)
    sizes = (heads, count, rows, width, rows // blocks, slots, global_ids.shape[0])
    head_rows = -(-(heads * slots + 1 + global_ids.shape[0]) // 16) * 16
    vmem = pl.BlockSpec(memory_space=pltpu.VMEM)
    anyspace = pl.BlockSpec(memory_space=pl.ANY)
    params = pltpu.CompilerParams(vmem_limit_bytes=KERNEL_VMEM)
    head_rows = -(-(heads * slots + 1 + global_ids.shape[0]) // 16) * 16
    a, b = pl.pallas_call(
        functools.partial(pack_kernel, sizes),
        out_shape=(
            pltpu.VMEM((2 * heads * rows, width), queries.dtype),
            pltpu.VMEM((2 * heads * rows + head_rows, width), queries.dtype),
        ),
        in_specs=[anyspace] * 6,
        out_specs=(vmem, vmem),
        scratch_shapes=[
            pltpu.SMEM(rand_ids.shape, jnp.int32),
            pltpu.SMEM(global_ids.shape, jnp.int32),
            pltpu.SemaphoreType.DMA((2 + 4 * heads,)),
        ],
    )(rand_ids, global_ids, keys, values, queries, grad_out)

    b_all = [b] + [exchanged(b, s * n_keys) for s in range(1, n_queries)]
    a_all = {0: a}
    for moves in key_moves(n_keys):
        for m, last in moves:
            a_all[m] = exchanged(a_all[m - last], last)
    a_all = [a_all[m] for m in range(n_keys)]
    lanes = n_queries * rows
    stat_rows = -(-3 * heads // 8) * 8
    order = [0] + [m for moves in key_moves(n_keys) for m in sorted(m for m, _ in moves)]
    a_all = near([a_all[m] for m in order])
    b_all = near(b_all)
    n_first = 1 + len(key_moves(n_keys)[0])
    stat, kept = None, []
    for here in (slice(0, n_first), slice(n_first, n_keys)):
        part = a_all[here]
        before = near([stat]) if kept else []
        stat, e, dp = pl.pallas_call(
            functools.partial(stats_kernel, sizes, order[here], n_queries),
            out_shape=(pltpu.VMEM((stat_rows, lanes), jnp.float32),)
            + (pltpu.VMEM((heads, len(part) * rows, lanes), jnp.float32),) * 2,
            compiler_params=params,
            in_specs=[vmem] * (len(part) + n_queries + len(before)),
            out_specs=(vmem,) * 3,
        )(*part, *b_all, *before)
        kept += ([] if kept else [stat]) + [e, dp]
    kept = near(kept)
    stats = [stat] + [exchanged(stat, s * n_keys) for s in range(1, n_queries)]
    sums = pl.pallas_call(
        functools.partial(partner_kernel, sizes, widths),
        out_shape=(pltpu.VMEM((2 * heads * rows, width), queries.dtype),) * (n_queries - 1),
        compiler_params=params,
        in_specs=[vmem] * (n_keys + 6),
        out_specs=(vmem,) * (n_queries - 1),
    )(*a_all, *near([stat]), *kept)
    sums = [exchanged(x, s * n_keys) for s, x in zip(range(1, n_queries), sums)]
    shapes = [pltpu.VMEM((2 * heads * rows, width), jnp.float32)]
    shapes += [pltpu.VMEM((2 * heads * rows, width), queries.dtype)] * (n_keys - 1)
    parts = []
    for picked in (slice(n_first, n_keys), slice(0, n_first)):
        got = pl.pallas_call(
            functools.partial(grads_kernel, sizes, widths, picked),
            out_shape=tuple(shapes[picked]),
            compiler_params=params,
            in_specs=[vmem] * (2 * n_queries + 5),
            out_specs=(vmem,) * len(shapes[picked]),
        )(*b_all, *near(stats), *kept)
        parts = [*got, *parts]
    parts = [parts[0]] + [exchanged(x, m) for m, x in zip(order[1:], parts[1:])]
    out = jax.ShapeDtypeStruct(queries.shape, queries.dtype)
    grad_queries = pl.pallas_call(
        functools.partial(queries_kernel, sizes, widths),
        out_shape=out,
        compiler_params=params,
        in_specs=[vmem] * (n_keys + 2 * n_queries + 4),
        out_specs=vmem,
    )(*a_all, *near(stats), *kept, *near(sums))
    buf = pltpu.VMEM(queries.shape, queries.dtype)
    grad_keys, grad_values = pl.pallas_call(
        functools.partial(sum_kernel, sizes, n_keys),
        out_shape=(out, out),
        compiler_params=params,
        in_specs=[vmem] * n_keys,
        out_specs=(anyspace,) * 2,
        scratch_shapes=[buf, buf, pltpu.SemaphoreType.DMA((2 * heads,))],
    )(*near(parts))
    return grad_queries, grad_keys, grad_values


def with_halo(value, sides, width):
    for axis, dim in sides:
        peers, length = (lax.axis_size(axis), value.shape[dim])
        up = [(i, (i + 1) % peers) for i in range(peers - 1)]
        down = [(j, i) for i, j in up]
        last = lax.slice_in_dim(value, length - width, length, axis=dim)
        initial = lax.slice_in_dim(value, 0, width, axis=dim)
        before = lax.ppermute(last, axis, up)
        after = lax.ppermute(initial, axis, down)
        value = jnp.concatenate([before, value, after], axis=dim)
    return value


def swapped(value, axis, distance):
    mask = 2**distance
    pairs = [(source, source ^ mask) for source in range(lax.axis_size(axis))]
    return lax.ppermute(value, axis, pairs)


def section_list(section_count):
    return list(range(section_count))


def routed(queries, keys, values, grad_out, rand_ids, global_ids):
    head_count, row_count, head_width = queries.shape
    block_count = rand_ids.shape[1]
    slot_count = rand_ids.shape[2]
    block_rows = row_count // block_count
    global_count = global_ids.shape[0]
    slot_total = 3 + global_count + slot_count
    device = lax.axis_index("seq")
    seq_count = lax.axis_size("seq")
    sections = section_list(seq_count.bit_length() - 1)
    score_scale = 1.0 / math.sqrt(head_width)
    key_vals = jnp.stack([keys, values])
    padded = with_halo(key_vals, (("seq", 2),), block_rows)
    padded_blocks = padded.reshape(2, head_count, block_count + 2, block_rows, head_width)
    window = jnp.stack(
        [
            padded_blocks[:, :, 0:block_count],
            padded_blocks[:, :, 1 : block_count + 1],
            padded_blocks[:, :, 2 : block_count + 2],
        ],
        3,
    )
    key_blocks = key_vals.reshape(2, head_count, block_count, block_rows, head_width)
    global_local = global_ids % block_count
    global_owner = global_ids // block_count
    owned = (global_owner == device).astype(jnp.float32)
    picked = jnp.take(key_blocks, global_local, axis=2).astype(jnp.float32)
    global_sum = lax.psum(picked * owned[None, None, :, None, None], "seq")
    global_kv = global_sum.astype(jnp.bfloat16)
    global_keys = jnp.broadcast_to(
        global_kv[:, :, None], (2, head_count, block_count, global_count, block_rows, head_width)
    )
    xor_masks = jnp.bitwise_xor(rand_ids[:, 0, :] // block_count, device)
    pieces = []
    for slot_index in range(slot_count):
        moving = key_vals
        for bit_index in sections:
            arrived = swapped(moving, "seq", bit_index)
            flag_now = jnp.right_shift(xor_masks[:, slot_index], bit_index) & 1 == 1
            moving = jnp.where(flag_now[None, :, None, None], arrived, moving)
        pieces.append(moving)
    routed = jnp.stack(pieces)
    routed_blocks = routed.reshape(slot_count, 2, head_count, block_count, block_rows, head_width)
    random_local = rand_ids % block_count
    local_onehot = (random_local[..., None] == jnp.arange(block_count, dtype=jnp.int32)).astype(
        jnp.bfloat16
    )
    random_keys = jnp.einsum(
        "hqjl,jchlbd->chqjbd", local_onehot, routed_blocks, preferred_element_type=jnp.float32
    ).astype(jnp.bfloat16)
    all_keys = jnp.concatenate([window, global_keys, random_keys], axis=3)
    key_list = all_keys[0].reshape(head_count, block_count, slot_total * block_rows, head_width)
    value_list = all_keys[1].reshape(head_count, block_count, slot_total * block_rows, head_width)
    block_range = jnp.arange(block_count, dtype=jnp.int32)
    left_valid = jnp.logical_not((block_range == 0) & (device == 0))
    right_valid = jnp.logical_not((block_range == block_count - 1) & (device == seq_count - 1))
    valid = jnp.concatenate(
        [
            left_valid[:, None],
            jnp.ones((block_count, 1), bool),
            right_valid[:, None],
            jnp.ones((block_count, global_count + slot_count), bool),
        ],
        1,
    )
    mask = jnp.repeat(valid, block_rows, axis=1)[None, :, None, :]
    query_blocks = queries.reshape(head_count, block_count, block_rows, head_width)
    grad_blocks = grad_out.reshape(head_count, block_count, block_rows, head_width)
    scores = (
        jnp.einsum("hnqd,hnkd->hnqk", query_blocks, key_list, preferred_element_type=jnp.float32)
        * score_scale
    )
    row_max = jnp.max(jnp.where(mask, scores, -1e30), -1)
    total = jnp.sum(jnp.where(mask, jnp.exp(scores - row_max[..., None]), 0.0), -1)
    log_total = row_max + jnp.log(total)
    probs = jnp.where(mask, jnp.exp(scores - log_total[..., None]), 0.0)
    probs_low = probs.astype(jnp.bfloat16)
    output = jnp.einsum(
        "hnqk,hnkd->hnqd", probs_low, value_list, preferred_element_type=jnp.float32
    )
    row_dot = jnp.sum(grad_blocks.astype(jnp.float32) * output, -1)
    grad_probs = jnp.einsum(
        "hnqd,hnkd->hnqk", grad_blocks, value_list, preferred_element_type=jnp.float32
    )
    scores_low = (probs * (grad_probs - row_dot[..., None])).astype(jnp.bfloat16)
    grad_query = score_scale * jnp.einsum(
        "hnqk,hnkd->hnqd", scores_low, key_list, preferred_element_type=jnp.float32
    )
    key_terms = score_scale * jnp.einsum(
        "hnqk,hnqd->hnkd", scores_low, query_blocks, preferred_element_type=jnp.float32
    )
    value_terms = jnp.einsum(
        "hnqk,hnqd->hnkd", probs_low, grad_blocks, preferred_element_type=jnp.float32
    )
    grads = jnp.stack([key_terms, value_terms]).reshape(
        2, head_count, block_count, slot_total, block_rows, head_width
    )
    no_pad = (0, 0)
    frame_sum = jnp.pad(grads[:, :, :, 0], (no_pad, no_pad, (0, 2), no_pad, no_pad))
    frame_sum = frame_sum + jnp.pad(grads[:, :, :, 1], (no_pad, no_pad, (1, 1), no_pad, no_pad))
    frame_sum = frame_sum + jnp.pad(grads[:, :, :, 2], (no_pad, no_pad, (2, 0), no_pad, no_pad))
    own_grads = frame_sum[:, :, 1 : block_count + 1]
    rim_parts = jnp.concatenate([frame_sum[:, :, 0], frame_sum[:, :, block_count + 1]], axis=2)
    rim_back = with_halo(rim_parts.astype(jnp.bfloat16), (("seq", 2),), block_rows).astype(
        rim_parts.dtype
    )
    own_grads = own_grads.at[:, :, 0].add(rim_back[:, :, 0:block_rows])
    own_grads = own_grads.at[:, :, block_count - 1].add(
        rim_back[:, :, 3 * block_rows : 4 * block_rows]
    )
    global_part = jnp.sum(grads[:, :, :, 3 : 3 + global_count], axis=2)
    global_total = lax.psum(global_part, "seq")
    global_onehot = (
        (global_local[:, None] == block_range[None, :]) & (global_owner == device)[:, None]
    ).astype(jnp.float32)
    own_grads = own_grads + jnp.einsum(
        "gn,chgbd->chnbd", global_onehot, global_total, precision=lax.Precision.HIGHEST
    )
    random_part = grads[:, :, :, 3 + global_count :]
    local_float = (random_local[..., None] == block_range).astype(jnp.float32)
    send_back = jnp.einsum(
        "hqjl,chqjbd->jchlbd", local_float, random_part, precision=lax.Precision.HIGHEST
    )
    send_back = send_back.astype(jnp.bfloat16).reshape(
        slot_count, 2, head_count, row_count, head_width
    )
    pieces = []
    for slot_index in range(slot_count):
        moving = send_back[slot_index]
        for bit_index in sections:
            arrived = swapped(moving, "seq", bit_index)
            flag_now = jnp.right_shift(xor_masks[:, slot_index], bit_index) & 1 == 1
            moving = jnp.where(flag_now[None, :, None, None], arrived, moving)
        pieces.append(moving)
    returned = jnp.stack(pieces)
    returned_sum = jnp.sum(returned.astype(jnp.float32), axis=0).reshape(
        2, head_count, block_count, block_rows, head_width
    )
    own_grads = own_grads + returned_sum
    grad_queries = grad_query.reshape(head_count, row_count, head_width).astype(jnp.bfloat16)
    grad_keys = own_grads[0].reshape(head_count, row_count, head_width).astype(jnp.bfloat16)
    grad_values = own_grads[1].reshape(head_count, row_count, head_width).astype(jnp.bfloat16)
    return (grad_queries, grad_keys, grad_values)


def on_device(queries, keys, values, grad_out, rand_ids, global_ids):
    count = lax.axis_size("seq")
    rows, width = queries.shape[1:]
    gathered_bytes = 4 * count * queries.size * queries.dtype.itemsize
    if gathered_bytes <= GATHER_BYTES and count & (count - 1) == 0 and count > GROUP and rows == width:
        return gathered(queries, keys, values, grad_out, rand_ids, global_ids)
    return routed(queries, keys, values, grad_out, rand_ids, global_ids)


def solution(mesh):
    in_specs = (
        P("head", "seq", None),
        P("head", "seq", None),
        P("head", "seq", None),
        P("head", "seq", None),
        P("head", "seq", None),
        P(),
    )
    out_specs = (P("head", "seq", None), P("head", "seq", None), P("head", "seq", None))
    return jax.shard_map(
        on_device, mesh=mesh, in_specs=in_specs, out_specs=out_specs, check_vma=False
    )
```
